32 devices in a mesh: face: 2 (over y), tx: 4 (over z), ty: 4 (over x, core).
Axes of the slice: x: 2, y: 2, z: 4, core: 2. Of those that a mesh axis runs over, the one named last changes fastest.
Arguments:
- probes: float32 [2, 4, 2, 6, 32, 32], P(None, None, 'face', None, 'tx', 'ty'), may hold values from -6 to 6
- background_wind: float32 [2, 2, 6, 32, 32], P(None, 'face', None, 'tx', 'ty'), may hold values from -6 to 6
- layer_mass: float32 [2, 6, 32, 32], P('face', None, 'tx', 'ty'), may hold values from 0.5 to 2
- trajectory_heat_factor: float32 [2, 6, 32, 32], P('face', None, 'tx', 'ty'), may hold values from 0.3 to 3
- spread: float32 [4, 2, 6, 32, 32], P(None, 'face', None, 'tx', 'ty'), may hold values from 0.5 to 2
- inverse_misfit_variance: float32 [4, 2, 6, 32, 32], P(None, 'face', None, 'tx', 'ty'), may hold values from 0.25 to 4
- face_links: int32 [6, 4, 7], replicated, may hold values from -1 to 5, as said below
Outputs:
- applied: float32 [2, 4, 2, 6, 32, 32], P(None, None, 'face', None, 'tx', 'ty')
The draws below stay inside these ranges and needn't reach their ends.
Inputs may be any that keep to these rules, and one draw needn't show every extreme that they name: `face_links`: the table describes the six panels of a cube, each with a right-handed frame: for panel f and edge e, the panel across it, the edge of that panel which touches f, whether the index along the shared edge runs the other way, and the matrix of entries -1, 0, 1 that carries vector components from that panel's frame into the frame of f.
All inputs are finite; a program needn't handle non-finite values.
Results may differ from the reference program's by a relative error of at most 0.00002.
Values sent between devices are 32-bit elements; how exact they have to be, the bound alone decides.
A program may use at most 64 MiB of HBM per device.

```python
import math
import jax
import jax.numpy as jnp

PROBES = 2
LEV = 2
SIDE = 32


def draw_face_links(key, part):
    centre = jnp.array([[1, 0, 0], [-1, 0, 0], [0, 1, 0], [0, -1, 0], [0, 0, 1], [0, 0, -1]], jnp.int32)
    across = jnp.array([[0, 1, 0], [0, 0, 1], [0, 0, 1], [1, 0, 0], [1, 0, 0], [0, 1, 0]], jnp.int32)
    upward = jnp.array([[0, 0, 1], [0, 1, 0], [1, 0, 0], [0, 0, 1], [0, 1, 0], [1, 0, 0]], jnp.int32)
    order = jax.random.permutation(jax.random.fold_in(key, 11), 6)
    quarter = jax.random.randint(jax.random.fold_in(key, 12), (6,), 0, 4)
    centre = centre[order]
    across = across[order]
    upward = upward[order]
    turned = quarter[:, None]
    new_across = jnp.where(turned == 0, across, jnp.where(turned == 1, upward, jnp.where(turned == 2, -across, -upward)))
    new_upward = jnp.where(turned == 0, upward, jnp.where(turned == 1, -across, jnp.where(turned == 2, -upward, across)))
    across = new_across
    upward = new_upward
    outward = jnp.stack([-across, across, -upward, upward], axis=1)
    along_edge = jnp.stack([upward, upward, across, across], axis=1)
    hits = jnp.all(outward[:, :, None, :] == centre[None, None, :, :], axis=-1)
    neighbour = jnp.sum(hits.astype(jnp.int32) * jnp.arange(6, dtype=jnp.int32), axis=-1)
    far_out = outward[neighbour]
    back_hits = jnp.all(far_out == centre[:, None, None, :], axis=-1).astype(jnp.int32)
    far_edge = jnp.sum(back_hits * jnp.arange(4, dtype=jnp.int32), axis=-1)
    far_along = jnp.sum(back_hits[..., None] * along_edge[neighbour], axis=2)
    reverse = (jnp.sum(along_edge * far_along, axis=-1) < 0).astype(jnp.int32)
    near_centre = centre[:, None, :]
    folding = near_centre + outward

    def carried(vectors):
        return vectors - jnp.sum(vectors * near_centre, axis=-1, keepdims=True) * folding

    def projected(vectors, basis):
        return jnp.sum(vectors * basis, axis=-1)
    far_across = carried(across[neighbour])
    far_upward = carried(upward[neighbour])
    near_across = across[:, None, :]
    near_upward = upward[:, None, :]
    table = jnp.stack([neighbour, far_edge, reverse, projected(far_across, near_across), projected(far_upward, near_across), projected(far_across, near_upward), projected(far_upward, near_upward)], axis=-1)
    return table.astype(jnp.int32)


def steps_of(key, extent, split, smallest, top_value):
    level = 1.0
    for position, blocks in split:
        steps = jax.random.uniform(jax.random.fold_in(jax.random.fold_in(key, 6), position), (blocks,), jnp.float32, smallest / len(split), top_value / len(split))
        level = level * jnp.repeat(jnp.exp(steps), extent[position] // blocks).reshape((-1,) + (1,) * (len(extent) - 1 - position))
    return level


def gaussian(stream_key, shape, scale, reach, cuts=(), held_as=jnp.bfloat16):
    values = jax.random.normal(stream_key, shape, jnp.float32) * scale
    if len(cuts) > 0:
        values = steps_of(stream_key, shape, cuts, -0.22, 0.18) * values
    return jnp.clip(values, min=-reach, max=reach).astype(held_as)


def setup_inputs(seed: int = 0) -> dict:
    splits = jax.random.split(jax.random.key(seed), 8)
    probes = gaussian(splits[0], (PROBES, 4, LEV, 6, SIDE, SIDE), 1.0, 6.0, ((2, 2), (4, 4), (5, 4)), jnp.float32)
    background_wind = gaussian(splits[1], (2, LEV, 6, SIDE, SIDE), 1.0, 6.0, ((1, 2), (3, 4), (4, 4)), jnp.float32)
    layer_mass = jnp.clip(jnp.exp(math.log(2.0) - 1.3862944 * jax.random.uniform(splits[2], (LEV, 6, SIDE, SIDE), jnp.float32) ** steps_of(splits[2], (LEV, 6, SIDE, SIDE), ((0, 2), (2, 4), (3, 4)), -0.2, 0.2)), 0.5, 2.0)
    trajectory_heat_factor = jnp.clip(jnp.exp(math.log(3.0) - 2.3025851 * jax.random.uniform(splits[3], (LEV, 6, SIDE, SIDE), jnp.float32) ** steps_of(splits[3], (LEV, 6, SIDE, SIDE), ((0, 2), (2, 4), (3, 4)), -0.2, 0.2)), 0.3, 3.0)
    spread = jnp.clip(jnp.exp(math.log(2.0) - 1.3862944 * jax.random.uniform(splits[4], (4, LEV, 6, SIDE, SIDE), jnp.float32) ** steps_of(splits[4], (4, LEV, 6, SIDE, SIDE), ((1, 2), (3, 4), (4, 4)), -0.2, 0.2)), 0.5, 2.0)
    inverse_misfit_variance = jnp.clip(jnp.exp(math.log(4.0) - 2.7725887 * jax.random.uniform(splits[5], (4, LEV, 6, SIDE, SIDE), jnp.float32) ** steps_of(splits[5], (4, LEV, 6, SIDE, SIDE), ((1, 2), (3, 4), (4, 4)), -0.2, 0.2)), 0.25, 4.0)
    face_links = draw_face_links(jax.random.fold_in(splits[7], 71), 0)
    return dict(probes=probes, background_wind=background_wind, layer_mass=layer_mass, trajectory_heat_factor=trajectory_heat_factor, spread=spread, inverse_misfit_variance=inverse_misfit_variance, face_links=face_links)


time_increment = 0.3
forward_layout = (('vector', 0), ('vector', 2), ('scalar', 4), ('scalar', 5))

def carry_pair(leading, trailing, entries):
    return (entries[0] * leading + entries[1] * trailing, entries[2] * leading + entries[3] * trailing)

def rotate_edge(edge_strip, matrix_codes, layout):
    matrix = matrix_codes.astype(edge_strip.dtype)
    entries = [matrix[:, column].reshape(1, 1, 6, 1) for column in range(4)]
    channels = [edge_strip[number] for number in range(edge_strip.shape[0])]
    for species, offset in layout:
        if species == 'vector':
            channels[offset], channels[offset + 1] = carry_pair(channels[offset], channels[offset + 1], entries)
        elif species == 'tensor':
            channels[offset], channels[offset + 1] = carry_pair(channels[offset], channels[offset + 1], entries)
            channels[offset + 2], channels[offset + 3] = carry_pair(channels[offset + 2], channels[offset + 3], entries)
            channels[offset], channels[offset + 2] = carry_pair(channels[offset], channels[offset + 2], entries)
            channels[offset + 1], channels[offset + 3] = carry_pair(channels[offset + 1], channels[offset + 3], entries)
    return jnp.stack(channels)

def orient(edge_rows, face_links, side, layout):
    source_face = face_links[:, side, 0]
    source_edge = face_links[:, side, 1]
    chosen = edge_rows[:, :, :, source_face, source_edge, :]
    flipped = (face_links[:, side, 2] == 1).reshape(1, 1, 1, 6, 1)
    chosen = jnp.where(flipped, chosen[..., ::-1], chosen)
    return rotate_edge(chosen, face_links[:, side, 3:7], layout)

def extend(fields, face_links, layout):
    edge_rows = jnp.stack([fields[..., 0, :], fields[..., -1, :], fields[..., :, 0], fields[..., :, -1]], axis=4)
    padded = jnp.pad(fields, ((0, 0), (0, 0), (0, 0), (0, 0), (1, 1), (1, 1)))
    padded = padded.at[..., 0, 1:-1].set(orient(edge_rows, face_links, 0, layout))
    padded = padded.at[..., -1, 1:-1].set(orient(edge_rows, face_links, 1, layout))
    padded = padded.at[..., 1:-1, 0].set(orient(edge_rows, face_links, 2, layout))
    padded = padded.at[..., 1:-1, -1].set(orient(edge_rows, face_links, 3, layout))
    return padded

def slopes(padded):
    east_slope_derivative = 0.5 * (padded[..., 2:, 1:-1] - padded[..., :-2, 1:-1])
    north_slope_derivative = 0.5 * (padded[..., 1:-1, 2:] - padded[..., 1:-1, :-2])
    return (east_slope_derivative, north_slope_derivative)

def tangent(normalised_state_array, background_wind, layer_mass, trajectory_heat_factor, face_links):
    west_east_wind_part, south_north_wind_speed, sheet_depth_state, sheet_warmth_state = (normalised_state_array[:, 0], normalised_state_array[:, 1], normalised_state_array[:, 2], normalised_state_array[:, 3])
    east_wind_speed, north_wind_speed = (background_wind[0], background_wind[1])
    ground_barometric_load = jnp.cumsum(sheet_depth_state, axis=1)
    gravity_potential_level = sheet_warmth_state + trajectory_heat_factor * ground_barometric_load
    east_mass_transport = east_wind_speed * sheet_depth_state + layer_mass * west_east_wind_part
    north_mass_transport = north_wind_speed * sheet_depth_state + layer_mass * south_north_wind_speed
    joined_state_arrays = jnp.stack([west_east_wind_part, south_north_wind_speed, east_mass_transport, north_mass_transport, sheet_warmth_state, gravity_potential_level])
    east_slope_derivative, north_slope_derivative = slopes(extend(joined_state_arrays, face_links, forward_layout))
    west_east_wind_after = west_east_wind_part - time_increment * (east_slope_derivative[5] + east_wind_speed * east_slope_derivative[0] + north_wind_speed * north_slope_derivative[0])
    south_north_wind_after = south_north_wind_speed - time_increment * (north_slope_derivative[5] + east_wind_speed * east_slope_derivative[1] + north_wind_speed * north_slope_derivative[1])
    depth_after_update = sheet_depth_state - time_increment * (east_slope_derivative[2] + north_slope_derivative[3])
    warmth_after_update = sheet_warmth_state - time_increment * (east_wind_speed * east_slope_derivative[4] + north_wind_speed * north_slope_derivative[4])
    return jnp.stack([west_east_wind_after, south_north_wind_after, depth_after_update, warmth_after_update], axis=1)

def reference(probes, background_wind, layer_mass, trajectory_heat_factor, spread, inverse_misfit_variance, face_links):
    normalised_state_array = spread[None] * probes

    def linear_step(perturbed):
        return tangent(perturbed, background_wind, layer_mass, trajectory_heat_factor, face_links)
    model_image, pullback = jax.vjp(linear_step, normalised_state_array)
    adjoint_out, = pullback(inverse_misfit_variance[None] * model_image)
    return probes + spread[None] * adjoint_out
```

```python
import functools

import jax
import jax.numpy as jnp
from jax import lax
from jax.experimental import pallas as pl
from jax.experimental.pallas import tpu as pltpu
from jax.sharding import PartitionSpec as P

MESH = pl.DeviceIdType.MESH
SUBLANES = 8
LANES = 128
VMEM_BYTES = 4 * 2**20

time_increment = 0.3
forward_layout = (("vector", 0), ("vector", 2), ("scalar", 4), ("scalar", 5))
adjoint_layout = (("tensor", 0), ("vector", 4), ("scalar", 6), ("vector", 7))


def padded_2(array, sides, width):
    for axis, dim in sides:
        devices, length = (lax.axis_size(axis), array.shape[dim])
        up = [(i, (i + 1) % devices) for i in range(devices - 1)]
        down = [(j, i) for i, j in up]
        last = lax.slice_in_dim(array, length - width, length, axis=dim)
        leading = lax.slice_in_dim(array, 0, width, axis=dim)
        before = lax.ppermute(last, axis, up)
        after = lax.ppermute(leading, axis, down)
        array = jnp.concatenate([before, array, after], axis=dim)
    return array


def carried_in(value, axis, join, neutral, backward):
    count, mine = (lax.axis_size(axis), lax.axis_index(axis))
    pieces = lax.all_gather(value, axis)
    if backward:
        pieces = pieces[::-1]
        mine = count - 1 - mine
    total = jnp.full_like(value, 0) + jnp.asarray(neutral, value.dtype)

    def hop(position, total):
        longer = join(total, pieces[position])
        return jnp.where(position < mine, longer, total)

    return lax.fori_loop(0, count - 1, hop, total)


def carry_pair(leading, trailing, entries):
    return (
        entries[0] * leading + entries[1] * trailing,
        entries[2] * leading + entries[3] * trailing,
    )


def rotate_edge(edge_strip, matrix_codes, layout):
    matrix = matrix_codes.astype(edge_strip.dtype)
    entries = [matrix[:, column].reshape(1, 1, 6, 1) for column in range(4)]
    channels = [edge_strip[number] for number in range(edge_strip.shape[0])]
    for species, offset in layout:
        if species == "vector":
            channels[offset], channels[offset + 1] = carry_pair(
                channels[offset], channels[offset + 1], entries
            )
        elif species == "tensor":
            channels[offset], channels[offset + 1] = carry_pair(
                channels[offset], channels[offset + 1], entries
            )
            channels[offset + 2], channels[offset + 3] = carry_pair(
                channels[offset + 2], channels[offset + 3], entries
            )
            channels[offset], channels[offset + 2] = carry_pair(
                channels[offset], channels[offset + 2], entries
            )
            channels[offset + 1], channels[offset + 3] = carry_pair(
                channels[offset + 1], channels[offset + 3], entries
            )
    return jnp.stack(channels)


def orient(edge_rows, face_links, side, layout):
    lines = edge_rows.reshape(edge_rows.shape[:3] + (-1, edge_rows.shape[5]))
    sides = edge_rows.shape[4]
    chosen = jnp.concatenate(
        [
            lax.dynamic_slice_in_dim(
                lines, face_links[f, side, 0] * sides + face_links[f, side, 1], 1, 3
            )
            for f in range(face_links.shape[0])
        ],
        axis=3,
    )
    flipped = (face_links[:, side, 2] == 1).reshape(1, 1, 1, 6, 1)
    chosen = jnp.where(flipped, chosen[..., ::-1], chosen)
    return rotate_edge(chosen, face_links[:, side, 3:7], layout)


def face_rows(fields):
    tile_row = lax.axis_index("tx")
    tile_column = lax.axis_index("ty")
    low_rows = jnp.where(tile_row == 0, fields[..., 0, :], 0.0)
    high_rows = jnp.where(tile_row == lax.axis_size("tx") - 1, fields[..., -1, :], 0.0)
    low_columns = jnp.where(tile_column == 0, fields[..., :, 0], 0.0)
    high_columns = jnp.where(tile_column == lax.axis_size("ty") - 1, fields[..., :, -1], 0.0)
    row_pair = jnp.stack([low_rows, high_rows], axis=4)
    column_pair = jnp.stack([low_columns, high_columns], axis=4)
    row_full = lax.psum(lax.all_gather(row_pair, "ty", axis=5, tiled=True), "tx")
    column_full = lax.psum(lax.all_gather(column_pair, "tx", axis=5, tiled=True), "ty")
    return jnp.concatenate([row_full, column_full], axis=4)


def extended_slopes(fields, face_links, layout):
    row_cells = fields.shape[4]
    column_cells = fields.shape[5]
    tile_row = lax.axis_index("tx")
    tile_column = lax.axis_index("ty")
    padded = padded_2(fields, (("tx", 4), ("ty", 5)), 1)
    edge_rows = face_rows(fields)
    western = lax.dynamic_slice_in_dim(
        orient(edge_rows, face_links, 0, layout), tile_column * column_cells, column_cells, 4
    )
    eastern = lax.dynamic_slice_in_dim(
        orient(edge_rows, face_links, 1, layout), tile_column * column_cells, column_cells, 4
    )
    southern = lax.dynamic_slice_in_dim(
        orient(edge_rows, face_links, 2, layout), tile_row * row_cells, row_cells, 4
    )
    northern = lax.dynamic_slice_in_dim(
        orient(edge_rows, face_links, 3, layout), tile_row * row_cells, row_cells, 4
    )
    row_number = lax.broadcasted_iota(jnp.int32, (row_cells, column_cells), 0)
    column_number = lax.broadcasted_iota(jnp.int32, (row_cells, column_cells), 1)
    first_row = (row_number == 0) & (tile_row == 0)
    last_row = (row_number == row_cells - 1) & (tile_row == lax.axis_size("tx") - 1)
    first_column = (column_number == 0) & (tile_column == 0)
    last_column = (column_number == column_cells - 1) & (tile_column == lax.axis_size("ty") - 1)
    east_slope_derivative = 0.5 * (padded[..., 2:, 1:-1] - padded[..., :-2, 1:-1])
    east_slope_derivative = (
        east_slope_derivative
        + jnp.where(last_row, 0.5 * eastern[..., None, :], 0.0)
        - jnp.where(first_row, 0.5 * western[..., None, :], 0.0)
    )
    north_slope_derivative = 0.5 * (padded[..., 1:-1, 2:] - padded[..., 1:-1, :-2])
    north_slope_derivative = (
        north_slope_derivative
        + jnp.where(last_column, 0.5 * northern[..., :, None], 0.0)
        - jnp.where(first_column, 0.5 * southern[..., :, None], 0.0)
    )
    return (east_slope_derivative, north_slope_derivative)


def pressure_of(sheet_depth_state):
    within = jnp.cumsum(sheet_depth_state, axis=1)
    totals_here = within[:, -1]
    underneath = carried_in(totals_here, "face", jnp.add, jnp.zeros_like(totals_here), False)
    return within + underneath[:, None]


def load_of(sensitivity):
    within = jnp.flip(jnp.cumsum(jnp.flip(sensitivity, 1), axis=1), 1)
    totals_here = within[:, 0]
    overhead = carried_in(totals_here, "face", jnp.add, jnp.zeros_like(totals_here), True)
    return within + overhead[:, None]


def body(
    probes,
    background_wind,
    layer_mass,
    trajectory_heat_factor,
    spread,
    inverse_misfit_variance,
    face_links,
):
    normalised_state_array = spread[None] * probes
    west_east_wind_part, south_north_wind_speed, sheet_depth_state, sheet_warmth_state = (
        normalised_state_array[:, 0],
        normalised_state_array[:, 1],
        normalised_state_array[:, 2],
        normalised_state_array[:, 3],
    )
    east_wind_speed, north_wind_speed = (background_wind[0], background_wind[1])
    ground_barometric_load = pressure_of(sheet_depth_state)
    gravity_potential_level = sheet_warmth_state + trajectory_heat_factor * ground_barometric_load
    east_mass_transport = east_wind_speed * sheet_depth_state + layer_mass * west_east_wind_part
    north_mass_transport = (
        north_wind_speed * sheet_depth_state + layer_mass * south_north_wind_speed
    )
    joined_state_arrays = jnp.stack(
        [
            west_east_wind_part,
            south_north_wind_speed,
            east_mass_transport,
            north_mass_transport,
            sheet_warmth_state,
            gravity_potential_level,
        ]
    )
    east_slope_derivative, north_slope_derivative = extended_slopes(
        joined_state_arrays, face_links, forward_layout
    )
    west_east_wind_after = west_east_wind_part - time_increment * (
        east_slope_derivative[5]
        + east_wind_speed * east_slope_derivative[0]
        + north_wind_speed * north_slope_derivative[0]
    )
    south_north_wind_after = south_north_wind_speed - time_increment * (
        north_slope_derivative[5]
        + east_wind_speed * east_slope_derivative[1]
        + north_wind_speed * north_slope_derivative[1]
    )
    depth_after_update = sheet_depth_state - time_increment * (
        east_slope_derivative[2] + north_slope_derivative[3]
    )
    warmth_after_update = sheet_warmth_state - time_increment * (
        east_wind_speed * east_slope_derivative[4] + north_wind_speed * north_slope_derivative[4]
    )
    zonal_cost = inverse_misfit_variance[0] * west_east_wind_after
    meridional_cost = inverse_misfit_variance[1] * south_north_wind_after
    thickness_cost = inverse_misfit_variance[2] * depth_after_update
    heat_misfit_penalty = inverse_misfit_variance[3] * warmth_after_update
    sensitive = jnp.stack(
        [
            east_wind_speed * zonal_cost,
            east_wind_speed * meridional_cost,
            north_wind_speed * zonal_cost,
            north_wind_speed * meridional_cost,
            zonal_cost,
            meridional_cost,
            thickness_cost,
            east_wind_speed * heat_misfit_penalty,
            north_wind_speed * heat_misfit_penalty,
        ]
    )
    east_slope_derivative, north_slope_derivative = extended_slopes(
        sensitive, face_links, adjoint_layout
    )
    geo_back = time_increment * (east_slope_derivative[4] + north_slope_derivative[5])
    flux_east_back = time_increment * east_slope_derivative[6]
    flux_north_back = time_increment * north_slope_derivative[6]
    zonal_back = (
        zonal_cost
        + time_increment * (east_slope_derivative[0] + north_slope_derivative[2])
        + layer_mass * flux_east_back
    )
    meridional_back = (
        meridional_cost
        + time_increment * (east_slope_derivative[1] + north_slope_derivative[3])
        + layer_mass * flux_north_back
    )
    warmth_back = (
        heat_misfit_penalty
        + time_increment * (east_slope_derivative[7] + north_slope_derivative[8])
        + geo_back
    )
    thickness_back = (
        thickness_cost
        + east_wind_speed * flux_east_back
        + north_wind_speed * flux_north_back
        + load_of(trajectory_heat_factor * geo_back)
    )
    adjoint_out = jnp.stack([zonal_back, meridional_back, thickness_back, warmth_back], axis=1)
    return probes + spread[None] * adjoint_out


def rolled(tile, shift, axis):
    return pltpu.roll(tile, shift % tile.shape[axis], axis)


def gathered(tile, index, axis):
    return jnp.take_along_axis(tile, index, axis=axis, mode="promise_in_bounds")


def block_transposed(tile, sub, inner):
    base = lax.broadcasted_iota(jnp.int32, tile.shape, 1) - inner
    skew = (inner - sub + SUBLANES) % SUBLANES
    tile = gathered(tile, base + skew, 1)
    tile = gathered(tile, skew, 0)
    return gathered(tile, base + (inner + sub) % SUBLANES, 1)


def block_reversed(tile, inner):
    lane = lax.broadcasted_iota(jnp.int32, tile.shape, 1)
    return gathered(tile, lane - inner + (SUBLANES - 1 - inner), 1)


def tile_kernel(
    count,
    faces,
    probes_hbm,
    wind_hbm,
    mass_hbm,
    heat_hbm,
    spread_hbm,
    variance_hbm,
    links_hbm,
    out_ref,
    probes_ref,
    wind_ref,
    mass_ref,
    heat_ref,
    spread_ref,
    variance_ref,
    links_ref,
    take_sem,
    strips_f,
    strips_a,
    halo_f,
    halo_a,
    slots_f,
    slots_a,
    ghosts,
    below_ref,
    above_ref,
    column_f,
    column_a,
    rows_f,
    rows_a,
    row_halo_f,
    row_halo_a,
    row_slots_f,
    row_slots_a,
    send_f,
    send_a,
    recv_halo_f,
    recv_halo_a,
    recv_slot_f,
    recv_slot_a,
    send_rows_f,
    send_rows_a,
    recv_row_halo_f,
    recv_row_halo_a,
    recv_row_slot_f,
    recv_row_slot_a,
    send_below,
    send_above,
    recv_below,
    recv_above,
):
    level = lax.axis_index("face")
    row = lax.axis_index("tx")
    column = lax.axis_index("ty")
    probe_count = probes_ref.shape[0]
    panels = probes_ref.shape[3]
    last = count - 1
    at = [row == 0, row == last, column == 0, column == last]
    on_row = at[0] | at[1]
    on_column = at[2] | at[3]
    corner = on_row & on_column
    middle = (on_row | on_column) & ~corner
    row_edge = jnp.where(at[0], 0, 1)
    column_edge = jnp.where(at[2], 2, 3)
    half = count // 2
    row_part = jnp.where(column < half, 0, 1)
    column_part = jnp.where(row < half, 0, 1)
    row_slot = row_edge * 2 + row_part
    column_slot = column_edge * 2 + column_part
    own_edge = jnp.where(on_row, row_edge, column_edge)
    own_slot = jnp.where(on_row, row_slot, column_slot)
    along = jnp.where(on_row, column, row)
    near = jnp.where(along < half, along, last - along)

    def slot_place(edge, part):
        segment = near if part == 0 else last - near
        return [(0, segment), (last, segment), (segment, 0), (segment, last)][edge]

    beside = [(row - 1, column), (row + 1, column), (row, column - 1), (row, column + 1)]
    corners = [(0, 0), (0, last), (last, 0), (last, last)]

    barrier = pltpu.get_barrier_semaphore()

    def greet(other, place):
        pl.semaphore_signal(
            barrier,
            inc=1,
            device_id={"face": other, "tx": place[0], "ty": place[1]},
            device_id_type=MESH,
        )

    for other in range(faces):
        for d in range(4):
            @pl.when(~at[d])
            def _():
                greet(other, beside[d])

        @pl.when(middle)
        def _():
            for slot in range(8):
                @pl.when((own_slot != slot) | (level != other))
                def _():
                    greet(other, slot_place(slot // 2, slot % 2))

        @pl.when(corner)
        def _():
            for place in corners:
                @pl.when((row != place[0]) | (column != place[1]) | (level != other))
                def _():
                    greet(other, place)

        @pl.when(level != other)
        def _():
            greet(other, (row, column))

    taken = [
        pltpu.make_async_copy(source, target, take_sem.at[i])
        for i, (source, target) in enumerate(
            (
                (probes_hbm, probes_ref),
                (spread_hbm, spread_ref),
                (wind_hbm, wind_ref),
                (mass_hbm, mass_ref),
                (heat_hbm, heat_ref),
                (variance_hbm, variance_ref),
                (links_hbm, links_ref),
            )
        )
    ]
    for copy in taken:
        copy.start()

    expected = (
        faces - 1 + jnp.where(middle, 8 * faces - 1, 0) + jnp.where(corner, 4 * faces - 1, 0)
    )
    for d in range(4):
        expected = expected + jnp.where(at[d], 0, faces)

    sub = lax.broadcasted_iota(jnp.int32, (SUBLANES, LANES), 0)
    lane = lax.broadcasted_iota(jnp.int32, (SUBLANES, LANES), 1)
    inner = lane % SUBLANES
    panel_of = (lane // SUBLANES) % panels

    def packed(tiles):
        width = LANES - SUBLANES * len(tiles)
        return jnp.concatenate(tiles + [jnp.zeros((SUBLANES, width), jnp.float32)], axis=1)

    def per_panel(load):
        return packed([load(f) for f in range(panels)] * probe_count)

    def per_probe(component):
        return packed(
            [
                probes_ref[p, component, 0, f]
                for p in range(probe_count)
                for f in range(panels)
            ]
        )

    def level_copy(other, source, target, send, recv):
        return pltpu.make_async_remote_copy(
            src_ref=source,
            dst_ref=target,
            send_sem=send,
            recv_sem=recv,
            device_id={"face": other},
            device_id_type=MESH,
        )

    def below_copy(other, slot):
        return level_copy(
            other, column_f, below_ref.at[slot], send_below.at[other], recv_below.at[slot]
        )

    def above_copy(other, slot):
        return level_copy(
            other, column_a, above_ref.at[slot], send_above.at[other], recv_above.at[slot]
        )

    nothing = jnp.zeros((SUBLANES, LANES), jnp.float32)

    def columns_of(y_fields):
        low = high = nothing
        for c, field in enumerate(y_fields):
            low = jnp.where(inner == c, rolled(field, c, 1), low)
            high = jnp.where(inner == c, rolled(field, c - (SUBLANES - 1), 1), high)
        return block_transposed(low, sub, inner), block_transposed(high, sub, inner)

    def write_strips(strips, x_fields, y_fields):
        low = high = nothing
        for c, field in enumerate(x_fields):
            low = jnp.where(sub == c, field[0:1, :], low)
            high = jnp.where(sub == c, field[SUBLANES - 1 : SUBLANES, :], high)
        strips[0] = low
        strips[1] = high
        strips[2], strips[3] = columns_of(y_fields)

    def strip_copy(source, target, send, recv, other, place):
        return pltpu.make_async_remote_copy(
            src_ref=source,
            dst_ref=target,
            send_sem=send,
            recv_sem=recv,
            device_id={"face": other, "tx": place[0], "ty": place[1]},
            device_id_type=MESH,
        )

    def each_send(buffers, act, target=None):
        strips, halo, slots, send, recv_halo, recv_slot = buffers
        across = target is not None
        other = target if across else level
        first_send = 12 * target if across else 0
        first_halo = 4 * level if across else 0
        first_slot = 8 * level if across else 0

        @pl.when(middle)
        def _():
            for slot in range(8):
                @pl.when((own_slot != slot) | across)
                def _():
                    act(
                        strip_copy(
                            strips.at[own_edge],
                            slots.at[first_slot + own_slot],
                            send.at[first_send + 4 + slot],
                            recv_slot.at[first_slot + own_slot],
                            other,
                            slot_place(slot // 2, slot % 2),
                        )
                    )

        @pl.when(corner)
        def _():
            for number, place in enumerate(corners):
                @pl.when((row != place[0]) | (column != place[1]) | across)
                def _():
                    for kind, (edge, slot) in enumerate(
                        ((row_edge, row_slot), (column_edge, column_slot))
                    ):
                        act(
                            strip_copy(
                                strips.at[edge],
                                slots.at[first_slot + slot],
                                send.at[first_send + 4 + number * 2 + kind],
                                recv_slot.at[first_slot + slot],
                                other,
                                place,
                            )
                        )

        for d in range(4):
            @pl.when(~at[d])
            def _():
                act(
                    strip_copy(
                        strips.at[d],
                        halo.at[first_halo + (d ^ 1)],
                        send.at[first_send + d],
                        recv_halo.at[first_halo + (d ^ 1)],
                        other,
                        beside[d],
                    )
                )

    def each_arrival(buffers, source=None):
        strips, halo, slots, send, recv_halo, recv_slot = buffers
        across = source is not None
        first_halo = 4 * source if across else 0
        first_slot = 8 * source if across else 0

        def arrival(target, semaphore):
            strip_copy(
                strips.at[0], target, send.at[0], semaphore, level, (row, column)
            ).wait_recv()

        for d in range(4):
            @pl.when(~at[d])
            def _():
                arrival(halo.at[first_halo + d], recv_halo.at[first_halo + d])

        @pl.when(on_row | on_column)
        def _():
            for slot in range(8):
                mine = (on_row & (row_slot == slot)) | (on_column & (column_slot == slot))

                @pl.when(~mine | across)
                def _():
                    arrival(slots.at[first_slot + slot], recv_slot.at[first_slot + slot])

    forward = (strips_f, halo_f, slots_f, send_f, recv_halo_f, recv_slot_f)
    adjoint = (strips_a, halo_a, slots_a, send_a, recv_halo_a, recv_slot_a)
    forward_rows = (
        rows_f, row_halo_f, row_slots_f, send_rows_f, recv_row_halo_f, recv_row_slot_f
    )
    adjoint_rows = (
        rows_a, row_halo_a, row_slots_a, send_rows_a, recv_row_halo_a, recv_row_slot_a
    )

    def keep_own(strips, slots):
        @pl.when(on_row)
        def _():
            slots[row_slot] = strips[row_edge]

        @pl.when(on_column)
        def _():
            slots[column_slot] = strips[column_edge]

    def with_levels(strip, rows, stride, index, is_adjoint):
        if is_adjoint:
            for other in range(1, faces):
                strip = jnp.where(sub == 4 + other, rows[stride * other + index], strip)
            return strip
        beneath = jnp.zeros((1, LANES), jnp.float32)
        for other in range(faces - 1):
            beneath = beneath + jnp.where(level > other, rows[stride * other + index], 0.0)
        return strip + jnp.where(sub == 4, rolled(strip, -1, 0) * beneath, 0.0)

    def start(copy):
        copy.start()

    def wait_send(copy):
        copy.wait_send()

    for copy in taken[:2]:
        copy.wait()
    probe_h = per_probe(2)
    spread_h = per_panel(lambda f: spread_ref[2, 0, f])
    h = spread_h * probe_h
    column_f[...] = h
    rows_f[0] = h[0:1, :]
    rows_f[1] = h[SUBLANES - 1 : SUBLANES, :]
    low, high = columns_of((h,))
    rows_f[2] = low[0:1, :]
    rows_f[3] = high[0:1, :]
    pl.semaphore_wait(barrier, expected)
    for other in range(1, faces):
        @pl.when(level < other)
        def _():
            each_send(forward_rows, start, other)
            below_copy(other, level).start()

    probe_z, probe_m, probe_t = per_probe(0), per_probe(1), per_probe(3)
    spread_z, spread_m, spread_t = [
        per_panel(lambda f, c=c: spread_ref[c, 0, f]) for c in (0, 1, 3)
    ]
    for copy in taken[2:5]:
        copy.wait()
    u, v = [per_panel(lambda f, c=c: wind_ref[c, 0, f]) for c in range(2)]
    mass = per_panel(lambda f: mass_ref[0, f])
    heat = per_panel(lambda f: heat_ref[0, f])
    z, m, t = spread_z * probe_z, spread_m * probe_m, spread_t * probe_t
    fx = u * h + mass * z
    fy = v * h + mass * m

    def ghost_across(slots, row_slots, edge, part, is_row, is_adjoint):
        strip = jnp.zeros((SUBLANES, LANES), jnp.float32)
        reverse = jnp.zeros((SUBLANES, LANES), jnp.int32)
        entries = [strip] * 4
        for f in range(panels):
            source = links_ref[f, edge, 0]
            flip = links_ref[f, edge, 2]
            slot = links_ref[f, edge, 1] * 2 + jnp.where(flip == 1, 1 - part, part)
            held = with_levels(slots[slot], row_slots, 8, slot, is_adjoint)
            shift = (SUBLANES * (f - source) + LANES) % LANES
            here = panel_of == f
            strip = jnp.where(here, pltpu.roll(held, shift, 1), strip)
            reverse = jnp.where(here, flip, reverse)
            entries = [
                jnp.where(here, links_ref[f, edge, 3 + i].astype(jnp.float32), entries[i])
                for i in range(4)
            ]
        strip = jnp.where(reverse == 1, block_reversed(strip, inner), strip)
        m0, m1, m2, m3 = entries
        normal = m0 + m1 if is_row else m2 + m3
        first = m0 * strip + m1 * rolled(strip, -1, 0)
        second = m3 * strip + m2 * rolled(strip, 1, 0)
        if is_adjoint:
            vectors = jnp.where(sub == 0, first, second) * normal
            return jnp.where(
                sub < 2, vectors, jnp.where(sub == 3, strip, normal * strip)
            )
        vectors = jnp.where(sub == 0, first, second)
        return jnp.where(sub < 2, vectors, jnp.where(sub == 2, normal * strip, strip))

    def make_ghosts(buffers, rows_buffers, is_adjoint):
        strips, halo, slots = buffers[:3]
        row_halo, row_slots = rows_buffers[1:3]
        for d in range(4):
            @pl.when(~at[d])
            def _():
                ghosts[d] = with_levels(halo[d], row_halo, 4, d, is_adjoint)

        @pl.when(on_row)
        def _():
            ghosts[row_edge] = ghost_across(
                slots, row_slots, row_edge, row_part, True, is_adjoint
            )

        @pl.when(on_column)
        def _():
            ghosts[column_edge] = ghost_across(
                slots, row_slots, column_edge, column_part, False, is_adjoint
            )

    def slopes_of(x_fields, y_fields):
        low, high = ghosts[0], ghosts[1]
        east = []
        for c, field in enumerate(x_fields):
            before = jnp.where(sub == 0, low[c : c + 1, :], rolled(field, 1, 0))
            after = jnp.where(sub == SUBLANES - 1, high[c : c + 1, :], rolled(field, -1, 0))
            east.append(0.5 * (after - before))
        low = block_transposed(ghosts[2], sub, inner)
        high = block_transposed(ghosts[3], sub, inner)
        north = []
        for c, field in enumerate(y_fields):
            before = jnp.where(inner == 0, rolled(low, -c, 1), rolled(field, 1, 1))
            after = jnp.where(
                inner == SUBLANES - 1, rolled(high, SUBLANES - 1 - c, 1), rolled(field, -1, 1)
            )
            north.append(0.5 * (after - before))
        return east, north

    geo = t + heat * h
    write_strips(strips_f, (z, m, fx, t, geo, heat), (z, m, fy, t, geo, heat))
    each_send(forward, start)
    keep_own(strips_f, slots_f)
    for copy in taken[5:]:
        copy.wait()
    var_z, var_m, var_h, var_t = [
        per_panel(lambda f, c=c: variance_ref[c, 0, f]) for c in range(4)
    ]
    each_arrival(forward)
    for other in range(faces - 1):
        @pl.when(level > other)
        def _():
            below_copy(other, other).wait_recv()
            each_arrival(forward_rows, other)

    for other in range(faces - 1):
        geo = geo + heat * jnp.where(level > other, below_ref[other], 0.0)
    make_ghosts(forward, forward_rows, False)
    east, north = slopes_of((z, m, fx, t, geo), (z, m, fy, t, geo))
    zc = var_z * (z - time_increment * (east[4] + u * east[0] + v * north[0]))
    mc = var_m * (m - time_increment * (north[4] + u * east[1] + v * north[1]))
    hc = var_h * (h - time_increment * (east[2] + north[2]))
    tc = var_t * (t - time_increment * (u * east[3] + v * north[3]))

    x_fields, y_fields = (u * zc, u * mc, zc, hc, u * tc), (v * zc, v * mc, mc, hc, v * tc)
    write_strips(strips_a, x_fields, y_fields)
    for d in range(4):
        rows_a[d] = strips_a[d][2:3, :]
    column_a[0], column_a[1], column_a[2] = zc, mc, heat
    for other in range(faces):
        @pl.when(level > other)
        def _():
            each_send(adjoint_rows, start, other)

    each_send(adjoint, start)
    for other in range(faces):
        @pl.when(level > other)
        def _():
            above_copy(other, level).start()

    keep_own(strips_a, slots_a)
    each_arrival(adjoint)
    for other in range(1, faces):
        @pl.when(level < other)
        def _():
            above_copy(other, other).wait_recv()
            each_arrival(adjoint_rows, other)

    make_ghosts(adjoint, adjoint_rows, True)
    above = [above_ref[other] for other in range(1, faces)]
    east, north = slopes_of(
        x_fields + tuple(tiles[0] for tiles in above),
        y_fields + tuple(tiles[1] for tiles in above),
    )
    geo_back = time_increment * (east[2] + north[2])
    load = heat * geo_back
    for other, tiles in enumerate(above, 1):
        upper = tiles[2] * (time_increment * (east[4 + other] + north[4 + other]))
        load = load + jnp.where(level < other, upper, 0.0)

    flux_east = time_increment * east[3]
    flux_north = time_increment * north[3]
    z_back = zc + time_increment * (east[0] + north[0]) + mass * flux_east
    m_back = mc + time_increment * (east[1] + north[1]) + mass * flux_north
    t_back = tc + time_increment * (east[4] + north[4]) + geo_back
    h_back = hc + u * flux_east + v * flux_north + load
    out_ref[0] = probe_z + spread_z * z_back
    out_ref[1] = probe_m + spread_m * m_back
    out_ref[2] = probe_h + spread_h * h_back
    out_ref[3] = probe_t + spread_t * t_back

    each_send(forward, wait_send)
    each_send(adjoint, wait_send)
    for other in range(faces):
        @pl.when(level < other)
        def _():
            each_send(forward_rows, wait_send, other)
            below_copy(other, level).wait_send()

        @pl.when(level > other)
        def _():
            each_send(adjoint_rows, wait_send, other)
            above_copy(other, level).wait_send()


def unpack_kernel(packed_ref, out_ref):
    probe_count, components, _, panels, _, _ = out_ref.shape
    for component in range(components):
        tile = packed_ref[component]
        for p in range(probe_count):
            for f in range(panels):
                start = (p * panels + f) * SUBLANES
                out_ref[p, component, 0, f] = tile[:, start : start + SUBLANES]


def fused(count, faces, *operands):
    tile = (SUBLANES, LANES)
    vmem = pl.BlockSpec(memory_space=pltpu.VMEM)
    whole = pl.BlockSpec(memory_space=pl.ANY)
    probes = operands[0]
    strips = pltpu.VMEM((4, *tile), jnp.float32)
    slots = pltpu.VMEM((8, *tile), jnp.float32)

    def edge_rows(number):
        return pltpu.VMEM((number, 1, LANES), jnp.float32)

    dma = pltpu.SemaphoreType.DMA
    packed = pl.pallas_call(
        functools.partial(tile_kernel, count, faces),
        out_shape=pltpu.VMEM((probes.shape[1], *tile), probes.dtype),
        in_specs=[whole] * len(operands),
        out_specs=vmem,
        scratch_shapes=[pltpu.VMEM(x.shape, x.dtype) for x in operands[:-1]]
        + [
            pltpu.SMEM(operands[-1].shape, operands[-1].dtype),
            dma((len(operands),)),
        ]
        + [strips] * 4
        + [slots] * 2
        + [strips]
        + [pltpu.VMEM((faces, *tile), jnp.float32), pltpu.VMEM((faces, 3, *tile), jnp.float32)]
        + [pltpu.VMEM(tile, jnp.float32), pltpu.VMEM((3, *tile), jnp.float32)]
        + [edge_rows(4)] * 2
        + [edge_rows(4 * faces)] * 2
        + [edge_rows(8 * faces)] * 2
        + [dma((12,))] * 2
        + [dma((4,))] * 2
        + [dma((8,))] * 2
        + [dma((12 * faces,))] * 2
        + [dma((4 * faces,))] * 2
        + [dma((8 * faces,))] * 2
        + [dma((faces,))] * 4,
        compiler_params=pltpu.CompilerParams(collective_id=0, has_side_effects=True),
    )(*operands)
    return pl.pallas_call(
        unpack_kernel,
        out_shape=jax.ShapeDtypeStruct(probes.shape, probes.dtype),
        in_specs=[vmem],
        out_specs=vmem,
        compiler_params=pltpu.CompilerParams(vmem_limit_bytes=VMEM_BYTES),
    )(packed)


def solution(mesh):
    count, faces = mesh.shape["tx"], mesh.shape["face"]

    def chosen(*operands):
        probe_count, _, levels, panels, rows, columns = operands[0].shape
        fits = (
            levels == 1
            and count == mesh.shape["ty"]
            and count % 2 == 0
            and rows == columns == SUBLANES
            and faces + 4 <= SUBLANES
            and probe_count * panels * SUBLANES < LANES
        )
        return fused(count, faces, *operands) if fits else body(*operands)

    return jax.shard_map(
        chosen,
        mesh=mesh,
        in_specs=(
            P(None, None, "face", None, "tx", "ty"),
            P(None, "face", None, "tx", "ty"),
            P("face", None, "tx", "ty"),
            P("face", None, "tx", "ty"),
            P(None, "face", None, "tx", "ty"),
            P(None, "face", None, "tx", "ty"),
            P(),
        ),
        out_specs=P(None, None, "face", None, "tx", "ty"),
        check_vma=False,
    )
```

```python
import functools

import jax
import jax.numpy as jnp
from jax import lax
from jax.experimental import pallas as pl
from jax.experimental.pallas import tpu as pltpu
from jax.sharding import PartitionSpec as P

MESH = pl.DeviceIdType.MESH
SUBLANES = 8
LANES = 128
VMEM_BYTES = 4 * 2**20

time_increment = 0.3
forward_layout = (("vector", 0), ("vector", 2), ("scalar", 4), ("scalar", 5))
adjoint_layout = (("tensor", 0), ("vector", 4), ("scalar", 6), ("vector", 7))


def padded_2(array, sides, width):
    for axis, dim in sides:
        devices, length = (lax.axis_size(axis), array.shape[dim])
        up = [(i, (i + 1) % devices) for i in range(devices - 1)]
        down = [(j, i) for i, j in up]
        last = lax.slice_in_dim(array, length - width, length, axis=dim)
        leading = lax.slice_in_dim(array, 0, width, axis=dim)
        before = lax.ppermute(last, axis, up)
        after = lax.ppermute(leading, axis, down)
        array = jnp.concatenate([before, array, after], axis=dim)
    return array


def carried_in(value, axis, join, neutral, backward):
    count, mine = (lax.axis_size(axis), lax.axis_index(axis))
    pieces = lax.all_gather(value, axis)
    if backward:
        pieces = pieces[::-1]
        mine = count - 1 - mine
    total = jnp.full_like(value, 0) + jnp.asarray(neutral, value.dtype)

    def hop(position, total):
        longer = join(total, pieces[position])
        return jnp.where(position < mine, longer, total)

    return lax.fori_loop(0, count - 1, hop, total)


def carry_pair(leading, trailing, entries):
    return (
        entries[0] * leading + entries[1] * trailing,
        entries[2] * leading + entries[3] * trailing,
    )


def rotate_edge(edge_strip, matrix_codes, layout):
    matrix = matrix_codes.astype(edge_strip.dtype)
    entries = [matrix[:, column].reshape(1, 1, 6, 1) for column in range(4)]
    channels = [edge_strip[number] for number in range(edge_strip.shape[0])]
    for species, offset in layout:
        if species == "vector":
            channels[offset], channels[offset + 1] = carry_pair(
                channels[offset], channels[offset + 1], entries
            )
        elif species == "tensor":
            channels[offset], channels[offset + 1] = carry_pair(
                channels[offset], channels[offset + 1], entries
            )
            channels[offset + 2], channels[offset + 3] = carry_pair(
                channels[offset + 2], channels[offset + 3], entries
            )
            channels[offset], channels[offset + 2] = carry_pair(
                channels[offset], channels[offset + 2], entries
            )
            channels[offset + 1], channels[offset + 3] = carry_pair(
                channels[offset + 1], channels[offset + 3], entries
            )
    return jnp.stack(channels)


def orient(edge_rows, face_links, side, layout):
    lines = edge_rows.reshape(edge_rows.shape[:3] + (-1, edge_rows.shape[5]))
    sides = edge_rows.shape[4]
    chosen = jnp.concatenate(
        [
            lax.dynamic_slice_in_dim(
                lines, face_links[f, side, 0] * sides + face_links[f, side, 1], 1, 3
            )
            for f in range(face_links.shape[0])
        ],
        axis=3,
    )
    flipped = (face_links[:, side, 2] == 1).reshape(1, 1, 1, 6, 1)
    chosen = jnp.where(flipped, chosen[..., ::-1], chosen)
    return rotate_edge(chosen, face_links[:, side, 3:7], layout)


def face_rows(fields):
    tile_row = lax.axis_index("tx")
    tile_column = lax.axis_index("ty")
    low_rows = jnp.where(tile_row == 0, fields[..., 0, :], 0.0)
    high_rows = jnp.where(tile_row == lax.axis_size("tx") - 1, fields[..., -1, :], 0.0)
    low_columns = jnp.where(tile_column == 0, fields[..., :, 0], 0.0)
    high_columns = jnp.where(tile_column == lax.axis_size("ty") - 1, fields[..., :, -1], 0.0)
    row_pair = jnp.stack([low_rows, high_rows], axis=4)
    column_pair = jnp.stack([low_columns, high_columns], axis=4)
    row_full = lax.psum(lax.all_gather(row_pair, "ty", axis=5, tiled=True), "tx")
    column_full = lax.psum(lax.all_gather(column_pair, "tx", axis=5, tiled=True), "ty")
    return jnp.concatenate([row_full, column_full], axis=4)


def extended_slopes(fields, face_links, layout):
    row_cells = fields.shape[4]
    column_cells = fields.shape[5]
    tile_row = lax.axis_index("tx")
    tile_column = lax.axis_index("ty")
    padded = padded_2(fields, (("tx", 4), ("ty", 5)), 1)
    edge_rows = face_rows(fields)
    western = lax.dynamic_slice_in_dim(
        orient(edge_rows, face_links, 0, layout), tile_column * column_cells, column_cells, 4
    )
    eastern = lax.dynamic_slice_in_dim(
        orient(edge_rows, face_links, 1, layout), tile_column * column_cells, column_cells, 4
    )
    southern = lax.dynamic_slice_in_dim(
        orient(edge_rows, face_links, 2, layout), tile_row * row_cells, row_cells, 4
    )
    northern = lax.dynamic_slice_in_dim(
        orient(edge_rows, face_links, 3, layout), tile_row * row_cells, row_cells, 4
    )
    row_number = lax.broadcasted_iota(jnp.int32, (row_cells, column_cells), 0)
    column_number = lax.broadcasted_iota(jnp.int32, (row_cells, column_cells), 1)
    first_row = (row_number == 0) & (tile_row == 0)
    last_row = (row_number == row_cells - 1) & (tile_row == lax.axis_size("tx") - 1)
    first_column = (column_number == 0) & (tile_column == 0)
    last_column = (column_number == column_cells - 1) & (tile_column == lax.axis_size("ty") - 1)
    east_slope_derivative = 0.5 * (padded[..., 2:, 1:-1] - padded[..., :-2, 1:-1])
    east_slope_derivative = (
        east_slope_derivative
        + jnp.where(last_row, 0.5 * eastern[..., None, :], 0.0)
        - jnp.where(first_row, 0.5 * western[..., None, :], 0.0)
    )
    north_slope_derivative = 0.5 * (padded[..., 1:-1, 2:] - padded[..., 1:-1, :-2])
    north_slope_derivative = (
        north_slope_derivative
        + jnp.where(last_column, 0.5 * northern[..., :, None], 0.0)
        - jnp.where(first_column, 0.5 * southern[..., :, None], 0.0)
    )
    return (east_slope_derivative, north_slope_derivative)


def pressure_of(sheet_depth_state):
    within = jnp.cumsum(sheet_depth_state, axis=1)
    totals_here = within[:, -1]
    underneath = carried_in(totals_here, "face", jnp.add, jnp.zeros_like(totals_here), False)
    return within + underneath[:, None]


def load_of(sensitivity):
    within = jnp.flip(jnp.cumsum(jnp.flip(sensitivity, 1), axis=1), 1)
    totals_here = within[:, 0]
    overhead = carried_in(totals_here, "face", jnp.add, jnp.zeros_like(totals_here), True)
    return within + overhead[:, None]


def body(
    probes,
    background_wind,
    layer_mass,
    trajectory_heat_factor,
    spread,
    inverse_misfit_variance,
    face_links,
):
    normalised_state_array = spread[None] * probes
    west_east_wind_part, south_north_wind_speed, sheet_depth_state, sheet_warmth_state = (
        normalised_state_array[:, 0],
        normalised_state_array[:, 1],
        normalised_state_array[:, 2],
        normalised_state_array[:, 3],
    )
    east_wind_speed, north_wind_speed = (background_wind[0], background_wind[1])
    ground_barometric_load = pressure_of(sheet_depth_state)
    gravity_potential_level = sheet_warmth_state + trajectory_heat_factor * ground_barometric_load
    east_mass_transport = east_wind_speed * sheet_depth_state + layer_mass * west_east_wind_part
    north_mass_transport = (
        north_wind_speed * sheet_depth_state + layer_mass * south_north_wind_speed
    )
    joined_state_arrays = jnp.stack(
        [
            west_east_wind_part,
            south_north_wind_speed,
            east_mass_transport,
            north_mass_transport,
            sheet_warmth_state,
            gravity_potential_level,
        ]
    )
    east_slope_derivative, north_slope_derivative = extended_slopes(
        joined_state_arrays, face_links, forward_layout
    )
    west_east_wind_after = west_east_wind_part - time_increment * (
        east_slope_derivative[5]
        + east_wind_speed * east_slope_derivative[0]
        + north_wind_speed * north_slope_derivative[0]
    )
    south_north_wind_after = south_north_wind_speed - time_increment * (
        north_slope_derivative[5]
        + east_wind_speed * east_slope_derivative[1]
        + north_wind_speed * north_slope_derivative[1]
    )
    depth_after_update = sheet_depth_state - time_increment * (
        east_slope_derivative[2] + north_slope_derivative[3]
    )
    warmth_after_update = sheet_warmth_state - time_increment * (
        east_wind_speed * east_slope_derivative[4] + north_wind_speed * north_slope_derivative[4]
    )
    zonal_cost = inverse_misfit_variance[0] * west_east_wind_after
    meridional_cost = inverse_misfit_variance[1] * south_north_wind_after
    thickness_cost = inverse_misfit_variance[2] * depth_after_update
    heat_misfit_penalty = inverse_misfit_variance[3] * warmth_after_update
    sensitive = jnp.stack(
        [
            east_wind_speed * zonal_cost,
            east_wind_speed * meridional_cost,
            north_wind_speed * zonal_cost,
            north_wind_speed * meridional_cost,
            zonal_cost,
            meridional_cost,
            thickness_cost,
            east_wind_speed * heat_misfit_penalty,
            north_wind_speed * heat_misfit_penalty,
        ]
    )
    east_slope_derivative, north_slope_derivative = extended_slopes(
        sensitive, face_links, adjoint_layout
    )
    geo_back = time_increment * (east_slope_derivative[4] + north_slope_derivative[5])
    flux_east_back = time_increment * east_slope_derivative[6]
    flux_north_back = time_increment * north_slope_derivative[6]
    zonal_back = (
        zonal_cost
        + time_increment * (east_slope_derivative[0] + north_slope_derivative[2])
        + layer_mass * flux_east_back
    )
    meridional_back = (
        meridional_cost
        + time_increment * (east_slope_derivative[1] + north_slope_derivative[3])
        + layer_mass * flux_north_back
    )
    warmth_back = (
        heat_misfit_penalty
        + time_increment * (east_slope_derivative[7] + north_slope_derivative[8])
        + geo_back
    )
    thickness_back = (
        thickness_cost
        + east_wind_speed * flux_east_back
        + north_wind_speed * flux_north_back
        + load_of(trajectory_heat_factor * geo_back)
    )
    adjoint_out = jnp.stack([zonal_back, meridional_back, thickness_back, warmth_back], axis=1)
    return probes + spread[None] * adjoint_out


def rolled(tile, shift, axis):
    return pltpu.roll(tile, shift % tile.shape[axis], axis)


def gathered(tile, index, axis):
    return jnp.take_along_axis(tile, index, axis=axis, mode="promise_in_bounds")


def tile_kernel(
    count,
    faces,
    probes_hbm,
    wind_hbm,
    mass_hbm,
    heat_hbm,
    spread_hbm,
    variance_hbm,
    links_hbm,
    out_ref,
    probes_ref,
    wind_ref,
    mass_ref,
    heat_ref,
    spread_ref,
    variance_ref,
    links_ref,
    take_sem,
    strips_f,
    strips_a,
    halo_f,
    halo_a,
    slots_f,
    slots_a,
    ghosts,
    below_ref,
    above_ref,
    column_f,
    column_a,
    rows_f,
    rows_a,
    row_halo_f,
    row_halo_a,
    row_slots_f,
    row_slots_a,
    send_f,
    send_a,
    recv_halo_f,
    recv_halo_a,
    recv_slot_f,
    recv_slot_a,
    send_rows_f,
    send_rows_a,
    recv_row_halo_f,
    recv_row_halo_a,
    recv_row_slot_f,
    recv_row_slot_a,
    send_below,
    send_above,
    recv_below,
    recv_above,
):
    level = lax.axis_index("face")
    row = lax.axis_index("tx")
    column = lax.axis_index("ty")
    probe_count = probes_ref.shape[0]
    panels = probes_ref.shape[3]
    last = count - 1
    at = [row == 0, row == last, column == 0, column == last]
    on_row = at[0] | at[1]
    on_column = at[2] | at[3]
    corner = on_row & on_column
    middle = (on_row | on_column) & ~corner
    row_edge = jnp.where(at[0], 0, 1)
    column_edge = jnp.where(at[2], 2, 3)
    half = count // 2
    row_part = jnp.where(column < half, 0, 1)
    column_part = jnp.where(row < half, 0, 1)
    row_slot = row_edge * 2 + row_part
    column_slot = column_edge * 2 + column_part
    own_edge = jnp.where(on_row, row_edge, column_edge)
    own_slot = jnp.where(on_row, row_slot, column_slot)
    along = jnp.where(on_row, column, row)
    near = jnp.where(along < half, along, last - along)

    def slot_place(edge, part):
        segment = near if part == 0 else last - near
        return [(0, segment), (last, segment), (segment, 0), (segment, last)][edge]

    beside = [(row - 1, column), (row + 1, column), (row, column - 1), (row, column + 1)]
    corners = [(0, 0), (0, last), (last, 0), (last, last)]

    barrier = pltpu.get_barrier_semaphore()

    def greet(other, place):
        pl.semaphore_signal(
            barrier,
            inc=1,
            device_id={"face": other, "tx": place[0], "ty": place[1]},
            device_id_type=MESH,
        )

    taken = [
        pltpu.make_async_copy(source, target, take_sem.at[i])
        for i, (source, target) in enumerate(
            (
                (probes_hbm, probes_ref),
                (spread_hbm, spread_ref),
                (wind_hbm, wind_ref),
                (mass_hbm, mass_ref),
                (heat_hbm, heat_ref),
                (variance_hbm, variance_ref),
                (links_hbm, links_ref),
            )
        )
    ]
    for copy in taken:
        copy.start()

    for other in range(faces):
        for d in range(4):
            @pl.when(~at[d])
            def _():
                greet(other, beside[d])

        @pl.when(middle)
        def _():
            for slot in range(8):
                @pl.when((own_slot != slot) | (level != other))
                def _():
                    greet(other, slot_place(slot // 2, slot % 2))

        @pl.when(corner)
        def _():
            for place in corners:
                @pl.when((row != place[0]) | (column != place[1]) | (level != other))
                def _():
                    greet(other, place)

        @pl.when(level != other)
        def _():
            greet(other, (row, column))

    expected = (
        faces - 1 + jnp.where(middle, 8 * faces - 1, 0) + jnp.where(corner, 4 * faces - 1, 0)
    )
    for d in range(4):
        expected = expected + jnp.where(at[d], 0, faces)

    sub = lax.broadcasted_iota(jnp.int32, (SUBLANES, LANES), 0)
    lane = lax.broadcasted_iota(jnp.int32, (SUBLANES, LANES), 1)
    inner = lane % SUBLANES
    panel_of = (lane // SUBLANES) % panels
    base = lane - inner
    skew = (inner - sub + SUBLANES) % SUBLANES
    unskew = base + (inner + sub) % SUBLANES

    def packed(tiles):
        width = LANES - SUBLANES * len(tiles)
        return jnp.concatenate(tiles + [jnp.zeros((SUBLANES, width), jnp.float32)], axis=1)

    def per_panel(load):
        return packed([load(f) for f in range(panels)] * probe_count)

    def per_probe(component):
        return packed(
            [
                probes_ref[p, component, 0, f]
                for p in range(probe_count)
                for f in range(panels)
            ]
        )

    def level_copy(other, source, target, send, recv):
        return pltpu.make_async_remote_copy(
            src_ref=source,
            dst_ref=target,
            send_sem=send,
            recv_sem=recv,
            device_id={"face": other},
            device_id_type=MESH,
        )

    def below_copy(other, slot):
        return level_copy(
            other, column_f, below_ref.at[slot], send_below.at[other], recv_below.at[slot]
        )

    def above_copy(other, slot):
        return level_copy(
            other, column_a, above_ref.at[slot], send_above.at[other], recv_above.at[slot]
        )

    nothing = jnp.zeros((SUBLANES, LANES), jnp.float32)

    def columns_of(y_fields):
        low = high = nothing
        for c, field in enumerate(y_fields):
            low = jnp.where(skew == c, gathered(field, base, 1), low)
            high = jnp.where(skew == c, gathered(field, base + (SUBLANES - 1), 1), high)
        return [gathered(gathered(tile, skew, 0), unskew, 1) for tile in (low, high)]

    def write_strips(strips, x_fields, y_fields):
        low = high = nothing
        for c, field in enumerate(x_fields):
            low = jnp.where(sub == c, field[0:1, :], low)
            high = jnp.where(sub == c, field[SUBLANES - 1 : SUBLANES, :], high)
        strips[0] = low
        strips[1] = high
        strips[2], strips[3] = columns_of(y_fields)

    def strip_copy(source, target, send, recv, other, place):
        return pltpu.make_async_remote_copy(
            src_ref=source,
            dst_ref=target,
            send_sem=send,
            recv_sem=recv,
            device_id={"face": other, "tx": place[0], "ty": place[1]},
            device_id_type=MESH,
        )

    def each_send(buffers, target=None):
        strips, halo, slots, send, recv_halo, recv_slot = buffers
        across = target is not None
        other = target if across else level
        first_send = 5 * target if across else 0
        first_halo = 4 * level if across else 0
        first_slot = 8 * level if across else 0
        group = level if across else 0

        @pl.when(middle)
        def _():
            for slot in range(8):
                @pl.when((own_slot != slot) | across)
                def _():
                    strip_copy(
                        strips.at[own_edge],
                        slots.at[first_slot + own_slot],
                        send.at[first_send + 4],
                        recv_slot.at[group],
                        other,
                        slot_place(slot // 2, slot % 2),
                    ).start()

        @pl.when(corner)
        def _():
            for place in corners:
                @pl.when((row != place[0]) | (column != place[1]) | across)
                def _():
                    for edge, slot in ((row_edge, row_slot), (column_edge, column_slot)):
                        strip_copy(
                            strips.at[edge],
                            slots.at[first_slot + slot],
                            send.at[first_send + 4],
                            recv_slot.at[group],
                            other,
                            place,
                        ).start()

        for d in range(4):
            @pl.when(~at[d])
            def _():
                strip_copy(
                    strips.at[d],
                    halo.at[first_halo + (d ^ 1)],
                    send.at[first_send + d],
                    recv_halo.at[first_halo + (d ^ 1)],
                    other,
                    beside[d],
                ).start()

    def each_wait(buffers, sent, other=None):
        strips, halo, slots, send, recv_halo, recv_slot = buffers
        across = other is not None
        first_send = 5 * other if across else 0
        first_halo = 4 * other if across else 0
        group = other if across else 0

        def ended(ref, send_sem, recv_sem):
            copy = strip_copy(ref, ref, send_sem, recv_sem, level, (row, column))
            if sent:
                copy.wait_send()
            else:
                copy.wait_recv()

        for d in range(4):
            @pl.when(~at[d])
            def _():
                ended(halo.at[0], send.at[first_send + d], recv_halo.at[first_halo + d])

        for role, number in ((middle, 8 if across else 7), (corner, 8 if across else 6)):
            @pl.when(role)
            def _():
                ended(
                    slots.at[pl.ds(0, number)], send.at[first_send + 4], recv_slot.at[group]
                )

    forward = (strips_f, halo_f, slots_f, send_f, recv_halo_f, recv_slot_f)
    adjoint = (strips_a, halo_a, slots_a, send_a, recv_halo_a, recv_slot_a)
    forward_rows = (
        rows_f, row_halo_f, row_slots_f, send_rows_f, recv_row_halo_f, recv_row_slot_f
    )
    adjoint_rows = (
        rows_a, row_halo_a, row_slots_a, send_rows_a, recv_row_halo_a, recv_row_slot_a
    )

    def keep_own(strips, slots):
        @pl.when(on_row)
        def _():
            slots[row_slot] = strips[row_edge]

        @pl.when(on_column)
        def _():
            slots[column_slot] = strips[column_edge]

    def with_levels(strip, rows, stride, index, is_adjoint):
        if is_adjoint:
            for other in range(1, faces):
                strip = jnp.where(sub == 4 + other, rows[stride * other + index], strip)
            return strip
        beneath = jnp.zeros((1, LANES), jnp.float32)
        for other in range(faces - 1):
            beneath = beneath + jnp.where(level > other, rows[stride * other + index], 0.0)
        return strip + jnp.where(sub == 4, rolled(strip, -1, 0) * beneath, 0.0)

    for copy in taken[:2]:
        copy.wait()
    probe_h = per_probe(2)
    spread_h = per_panel(lambda f: spread_ref[2, 0, f])
    h = spread_h * probe_h
    column_f[...] = h
    rows_f[0] = h[0:1, :]
    rows_f[1] = h[SUBLANES - 1 : SUBLANES, :]
    low, high = columns_of((h,))
    rows_f[2] = low[0:1, :]
    rows_f[3] = high[0:1, :]
    probe_z, probe_m, probe_t = per_probe(0), per_probe(1), per_probe(3)
    spread_z, spread_m, spread_t = [
        per_panel(lambda f, c=c: spread_ref[c, 0, f]) for c in (0, 1, 3)
    ]
    for copy in taken[2:5]:
        copy.wait()
    u, v = [per_panel(lambda f, c=c: wind_ref[c, 0, f]) for c in range(2)]
    mass = per_panel(lambda f: mass_ref[0, f])
    heat = per_panel(lambda f: heat_ref[0, f])
    z, m, t = spread_z * probe_z, spread_m * probe_m, spread_t * probe_t
    fx = u * h + mass * z
    fy = v * h + mass * m

    def links_of(edge, part, is_row):
        zero = jnp.zeros((SUBLANES, LANES), jnp.int32)
        source = flip = slot = normal = tangent = zero
        for f in range(panels):
            here = panel_of == f
            entries = [links_ref[f, edge, 3 + i] for i in range(4)]
            first, second = entries[0] + entries[1], entries[2] + entries[3]
            turned = links_ref[f, edge, 2]
            held = links_ref[f, edge, 1] * 2 + jnp.where(turned == 1, 1 - part, part)
            source = jnp.where(here, links_ref[f, edge, 0], source)
            flip = jnp.where(here, turned, flip)
            slot = jnp.where(here, held, slot)
            normal = jnp.where(here, first if is_row else second, normal)
            tangent = jnp.where(here, second if is_row else first, tangent)
        along = inner if is_row else skew
        index = base + SUBLANES * (source - panel_of)
        index = index + jnp.where(flip == 1, SUBLANES - 1 - along, along)
        index = jnp.where(lane < SUBLANES * panels * probe_count, index, lane)
        normal, tangent = normal.astype(jnp.float32), tangent.astype(jnp.float32)
        ahead = jnp.where(sub == 1, tangent, jnp.where((sub == 0) | (sub == 2), normal, 1.0))
        back = jnp.where(
            sub == 1, normal * tangent, jnp.where((sub == 0) | (sub == 3), 1.0, normal)
        )
        return index, slot, ahead, back

    def ghost_across(slots, row_slots, links, is_adjoint):
        index, slot, ahead, back = links
        strip = nothing
        for number in range(8):
            held = with_levels(slots[number], row_slots, 8, number, is_adjoint)
            strip = jnp.where(slot == number, gathered(held, index, 1), strip)
        return strip * (back if is_adjoint else ahead)

    def make_ghosts(buffers, rows_buffers, is_adjoint):
        strips, halo, slots = buffers[:3]
        row_halo, row_slots = rows_buffers[1:3]
        for d in range(4):
            @pl.when(~at[d])
            def _():
                strip = with_levels(halo[d], row_halo, 4, d, is_adjoint)
                ghosts[d] = strip if d < 2 else gathered(strip, base + skew, 1)

        @pl.when(on_row)
        def _():
            ghosts[row_edge] = ghost_across(slots, row_slots, row_links, is_adjoint)

        @pl.when(on_column)
        def _():
            ghosts[column_edge] = ghost_across(slots, row_slots, column_links, is_adjoint)

    def slopes_of(x_fields, y_fields):
        low, high = ghosts[0], ghosts[1]
        east = []
        for c, field in enumerate(x_fields):
            before = jnp.where(sub == 0, low[c : c + 1, :], rolled(field, 1, 0))
            after = jnp.where(sub == SUBLANES - 1, high[c : c + 1, :], rolled(field, -1, 0))
            east.append(0.5 * (after - before))
        low, high = gathered(ghosts[2], skew, 0), gathered(ghosts[3], skew, 0)
        north = []
        for c, field in enumerate(y_fields):
            place = base + (sub + c) % SUBLANES
            before = jnp.where(inner == 0, gathered(low, place, 1), rolled(field, 1, 1))
            after = jnp.where(
                inner == SUBLANES - 1, gathered(high, place, 1), rolled(field, -1, 1)
            )
            north.append(0.5 * (after - before))
        return east, north

    geo = t + heat * h
    write_strips(strips_f, (z, m, fx, t, geo, heat), (m, z, fy, t, geo, heat))
    pl.semaphore_wait(barrier, expected)
    for other in range(1, faces):
        @pl.when(level < other)
        def _():
            each_send(forward_rows, other)
            below_copy(other, level).start()
    each_send(forward)

    keep_own(strips_f, slots_f)
    for copy in taken[5:]:
        copy.wait()
    var_z, var_m, var_h, var_t = [
        per_panel(lambda f, c=c: variance_ref[c, 0, f]) for c in range(4)
    ]
    row_links = links_of(row_edge, row_part, True)
    column_links = links_of(column_edge, column_part, False)
    each_wait(forward, False)
    for other in range(faces - 1):
        @pl.when(level > other)
        def _():
            below_copy(other, other).wait_recv()
            each_wait(forward_rows, False, other)

    for other in range(faces - 1):
        geo = geo + heat * jnp.where(level > other, below_ref[other], 0.0)
    make_ghosts(forward, forward_rows, False)
    east, north = slopes_of((z, m, fx, t, geo), (m, z, fy, t, geo))
    zc = var_z * (z - time_increment * (east[4] + u * east[0] + v * north[1]))
    mc = var_m * (m - time_increment * (north[4] + u * east[1] + v * north[0]))
    hc = var_h * (h - time_increment * (east[2] + north[2]))
    tc = var_t * (t - time_increment * (u * east[3] + v * north[3]))

    x_fields, y_fields = (u * zc, u * mc, zc, hc, u * tc), (v * mc, v * zc, mc, hc, v * tc)
    write_strips(strips_a, x_fields, y_fields)
    for d in range(4):
        rows_a[d] = strips_a[d][2:3, :]
    column_a[0], column_a[1], column_a[2] = zc, mc, heat
    for other in range(faces):
        @pl.when(level > other)
        def _():
            each_send(adjoint_rows, other)
            above_copy(other, level).start()
    each_send(adjoint)

    keep_own(strips_a, slots_a)
    each_wait(forward, True)
    each_wait(adjoint, True)
    for other in range(faces):
        @pl.when(level < other)
        def _():
            each_wait(forward_rows, True, other)
            below_copy(other, level).wait_send()

        @pl.when(level > other)
        def _():
            each_wait(adjoint_rows, True, other)
            above_copy(other, level).wait_send()

    each_wait(adjoint, False)
    for other in range(1, faces):
        @pl.when(level < other)
        def _():
            above_copy(other, other).wait_recv()
            each_wait(adjoint_rows, False, other)

    make_ghosts(adjoint, adjoint_rows, True)
    above = [above_ref[other] for other in range(1, faces)]
    east, north = slopes_of(
        x_fields + tuple(tiles[0] for tiles in above),
        y_fields + tuple(tiles[1] for tiles in above),
    )
    geo_back = time_increment * (east[2] + north[2])
    load = heat * geo_back
    for other, tiles in enumerate(above, 1):
        upper = tiles[2] * (time_increment * (east[4 + other] + north[4 + other]))
        load = load + jnp.where(level < other, upper, 0.0)

    flux_east = time_increment * east[3]
    flux_north = time_increment * north[3]
    z_back = zc + time_increment * (east[0] + north[1]) + mass * flux_east
    m_back = mc + time_increment * (east[1] + north[0]) + mass * flux_north
    t_back = tc + time_increment * (east[4] + north[4]) + geo_back
    h_back = hc + u * flux_east + v * flux_north + load
    out_ref[0] = probe_z + spread_z * z_back
    out_ref[1] = probe_m + spread_m * m_back
    out_ref[2] = probe_h + spread_h * h_back
    out_ref[3] = probe_t + spread_t * t_back


def unpack_kernel(packed_ref, out_ref):
    probe_count, components, _, panels, _, _ = out_ref.shape
    for component in range(components):
        tile = packed_ref[component]
        for p in range(probe_count):
            for f in range(panels):
                start = (p * panels + f) * SUBLANES
                out_ref[p, component, 0, f] = tile[:, start : start + SUBLANES]


def fused(count, faces, *operands):
    tile = (SUBLANES, LANES)
    vmem = pl.BlockSpec(memory_space=pltpu.VMEM)
    whole = pl.BlockSpec(memory_space=pl.ANY)
    probes = operands[0]
    strips = pltpu.VMEM((4, *tile), jnp.float32)
    slots = pltpu.VMEM((8, *tile), jnp.float32)

    def edge_rows(number):
        return pltpu.VMEM((number, 1, LANES), jnp.float32)

    dma = pltpu.SemaphoreType.DMA
    packed = pl.pallas_call(
        functools.partial(tile_kernel, count, faces),
        out_shape=pltpu.VMEM((probes.shape[1], *tile), probes.dtype),
        in_specs=[whole] * len(operands),
        out_specs=vmem,
        scratch_shapes=[pltpu.VMEM(x.shape, x.dtype) for x in operands[:-1]]
        + [
            pltpu.SMEM(operands[-1].shape, operands[-1].dtype),
            dma((len(operands),)),
        ]
        + [strips] * 4
        + [slots] * 2
        + [strips]
        + [pltpu.VMEM((faces, *tile), jnp.float32), pltpu.VMEM((faces, 3, *tile), jnp.float32)]
        + [pltpu.VMEM(tile, jnp.float32), pltpu.VMEM((3, *tile), jnp.float32)]
        + [edge_rows(4)] * 2
        + [edge_rows(4 * faces)] * 2
        + [edge_rows(8 * faces)] * 2
        + [dma((5,))] * 2
        + [dma((4,))] * 2
        + [dma((1,))] * 2
        + [dma((5 * faces,))] * 2
        + [dma((4 * faces,))] * 2
        + [dma((faces,))] * 2
        + [dma((faces,))] * 4,
        compiler_params=pltpu.CompilerParams(collective_id=0, has_side_effects=True),
    )(*operands)
    return pl.pallas_call(
        unpack_kernel,
        out_shape=jax.ShapeDtypeStruct(probes.shape, probes.dtype),
        in_specs=[vmem],
        out_specs=vmem,
        compiler_params=pltpu.CompilerParams(vmem_limit_bytes=VMEM_BYTES),
    )(packed)


def solution(mesh):
    count, faces = mesh.shape["tx"], mesh.shape["face"]

    def chosen(*operands):
        probe_count, _, levels, panels, rows, columns = operands[0].shape
        fits = (
            levels == 1
            and count == mesh.shape["ty"]
            and count % 2 == 0
            and rows == columns == SUBLANES
            and faces + 4 <= SUBLANES
            and probe_count * panels * SUBLANES < LANES
        )
        return fused(count, faces, *operands) if fits else body(*operands)

    return jax.shard_map(
        chosen,
        mesh=mesh,
        in_specs=(
            P(None, None, "face", None, "tx", "ty"),
            P(None, "face", None, "tx", "ty"),
            P("face", None, "tx", "ty"),
            P("face", None, "tx", "ty"),
            P(None, "face", None, "tx", "ty"),
            P(None, "face", None, "tx", "ty"),
            P(),
        ),
        out_specs=P(None, None, "face", None, "tx", "ty"),
        check_vma=False,
    )
```

```python
import functools

import jax
import jax.numpy as jnp
from jax import lax
from jax.experimental import pallas as pl
from jax.experimental.pallas import tpu as pltpu
from jax.sharding import PartitionSpec as P

MESH = pl.DeviceIdType.MESH
SUBLANES = 8
LANES = 128
VMEM_BYTES = 4 * 2**20

time_increment = 0.3
forward_layout = (("vector", 0), ("vector", 2), ("scalar", 4), ("scalar", 5))
adjoint_layout = (("tensor", 0), ("vector", 4), ("scalar", 6), ("vector", 7))


def padded_2(array, sides, width):
    for axis, dim in sides:
        devices, length = (lax.axis_size(axis), array.shape[dim])
        up = [(i, (i + 1) % devices) for i in range(devices - 1)]
        down = [(j, i) for i, j in up]
        last = lax.slice_in_dim(array, length - width, length, axis=dim)
        leading = lax.slice_in_dim(array, 0, width, axis=dim)
        before = lax.ppermute(last, axis, up)
        after = lax.ppermute(leading, axis, down)
        array = jnp.concatenate([before, array, after], axis=dim)
    return array


def carried_in(value, axis, join, neutral, backward):
    count, mine = (lax.axis_size(axis), lax.axis_index(axis))
    pieces = lax.all_gather(value, axis)
    if backward:
        pieces = pieces[::-1]
        mine = count - 1 - mine
    total = jnp.full_like(value, 0) + jnp.asarray(neutral, value.dtype)

    def hop(position, total):
        longer = join(total, pieces[position])
        return jnp.where(position < mine, longer, total)

    return lax.fori_loop(0, count - 1, hop, total)


def carry_pair(leading, trailing, entries):
    return (
        entries[0] * leading + entries[1] * trailing,
        entries[2] * leading + entries[3] * trailing,
    )


def rotate_edge(edge_strip, matrix_codes, layout):
    matrix = matrix_codes.astype(edge_strip.dtype)
    entries = [matrix[:, column].reshape(1, 1, 6, 1) for column in range(4)]
    channels = [edge_strip[number] for number in range(edge_strip.shape[0])]
    for species, offset in layout:
        if species == "vector":
            channels[offset], channels[offset + 1] = carry_pair(
                channels[offset], channels[offset + 1], entries
            )
        elif species == "tensor":
            channels[offset], channels[offset + 1] = carry_pair(
                channels[offset], channels[offset + 1], entries
            )
            channels[offset + 2], channels[offset + 3] = carry_pair(
                channels[offset + 2], channels[offset + 3], entries
            )
            channels[offset], channels[offset + 2] = carry_pair(
                channels[offset], channels[offset + 2], entries
            )
            channels[offset + 1], channels[offset + 3] = carry_pair(
                channels[offset + 1], channels[offset + 3], entries
            )
    return jnp.stack(channels)


def orient(edge_rows, face_links, side, layout):
    lines = edge_rows.reshape(edge_rows.shape[:3] + (-1, edge_rows.shape[5]))
    sides = edge_rows.shape[4]
    chosen = jnp.concatenate(
        [
            lax.dynamic_slice_in_dim(
                lines, face_links[f, side, 0] * sides + face_links[f, side, 1], 1, 3
            )
            for f in range(face_links.shape[0])
        ],
        axis=3,
    )
    flipped = (face_links[:, side, 2] == 1).reshape(1, 1, 1, 6, 1)
    chosen = jnp.where(flipped, chosen[..., ::-1], chosen)
    return rotate_edge(chosen, face_links[:, side, 3:7], layout)


def face_rows(fields):
    tile_row = lax.axis_index("tx")
    tile_column = lax.axis_index("ty")
    low_rows = jnp.where(tile_row == 0, fields[..., 0, :], 0.0)
    high_rows = jnp.where(tile_row == lax.axis_size("tx") - 1, fields[..., -1, :], 0.0)
    low_columns = jnp.where(tile_column == 0, fields[..., :, 0], 0.0)
    high_columns = jnp.where(tile_column == lax.axis_size("ty") - 1, fields[..., :, -1], 0.0)
    row_pair = jnp.stack([low_rows, high_rows], axis=4)
    column_pair = jnp.stack([low_columns, high_columns], axis=4)
    row_full = lax.psum(lax.all_gather(row_pair, "ty", axis=5, tiled=True), "tx")
    column_full = lax.psum(lax.all_gather(column_pair, "tx", axis=5, tiled=True), "ty")
    return jnp.concatenate([row_full, column_full], axis=4)


def extended_slopes(fields, face_links, layout):
    row_cells = fields.shape[4]
    column_cells = fields.shape[5]
    tile_row = lax.axis_index("tx")
    tile_column = lax.axis_index("ty")
    padded = padded_2(fields, (("tx", 4), ("ty", 5)), 1)
    edge_rows = face_rows(fields)
    western = lax.dynamic_slice_in_dim(
        orient(edge_rows, face_links, 0, layout), tile_column * column_cells, column_cells, 4
    )
    eastern = lax.dynamic_slice_in_dim(
        orient(edge_rows, face_links, 1, layout), tile_column * column_cells, column_cells, 4
    )
    southern = lax.dynamic_slice_in_dim(
        orient(edge_rows, face_links, 2, layout), tile_row * row_cells, row_cells, 4
    )
    northern = lax.dynamic_slice_in_dim(
        orient(edge_rows, face_links, 3, layout), tile_row * row_cells, row_cells, 4
    )
    row_number = lax.broadcasted_iota(jnp.int32, (row_cells, column_cells), 0)
    column_number = lax.broadcasted_iota(jnp.int32, (row_cells, column_cells), 1)
    first_row = (row_number == 0) & (tile_row == 0)
    last_row = (row_number == row_cells - 1) & (tile_row == lax.axis_size("tx") - 1)
    first_column = (column_number == 0) & (tile_column == 0)
    last_column = (column_number == column_cells - 1) & (tile_column == lax.axis_size("ty") - 1)
    east_slope_derivative = 0.5 * (padded[..., 2:, 1:-1] - padded[..., :-2, 1:-1])
    east_slope_derivative = (
        east_slope_derivative
        + jnp.where(last_row, 0.5 * eastern[..., None, :], 0.0)
        - jnp.where(first_row, 0.5 * western[..., None, :], 0.0)
    )
    north_slope_derivative = 0.5 * (padded[..., 1:-1, 2:] - padded[..., 1:-1, :-2])
    north_slope_derivative = (
        north_slope_derivative
        + jnp.where(last_column, 0.5 * northern[..., :, None], 0.0)
        - jnp.where(first_column, 0.5 * southern[..., :, None], 0.0)
    )
    return (east_slope_derivative, north_slope_derivative)


def pressure_of(sheet_depth_state):
    within = jnp.cumsum(sheet_depth_state, axis=1)
    totals_here = within[:, -1]
    underneath = carried_in(totals_here, "face", jnp.add, jnp.zeros_like(totals_here), False)
    return within + underneath[:, None]


def load_of(sensitivity):
    within = jnp.flip(jnp.cumsum(jnp.flip(sensitivity, 1), axis=1), 1)
    totals_here = within[:, 0]
    overhead = carried_in(totals_here, "face", jnp.add, jnp.zeros_like(totals_here), True)
    return within + overhead[:, None]


def body(
    probes,
    background_wind,
    layer_mass,
    trajectory_heat_factor,
    spread,
    inverse_misfit_variance,
    face_links,
):
    normalised_state_array = spread[None] * probes
    west_east_wind_part, south_north_wind_speed, sheet_depth_state, sheet_warmth_state = (
        normalised_state_array[:, 0],
        normalised_state_array[:, 1],
        normalised_state_array[:, 2],
        normalised_state_array[:, 3],
    )
    east_wind_speed, north_wind_speed = (background_wind[0], background_wind[1])
    ground_barometric_load = pressure_of(sheet_depth_state)
    gravity_potential_level = sheet_warmth_state + trajectory_heat_factor * ground_barometric_load
    east_mass_transport = east_wind_speed * sheet_depth_state + layer_mass * west_east_wind_part
    north_mass_transport = (
        north_wind_speed * sheet_depth_state + layer_mass * south_north_wind_speed
    )
    joined_state_arrays = jnp.stack(
        [
            west_east_wind_part,
            south_north_wind_speed,
            east_mass_transport,
            north_mass_transport,
            sheet_warmth_state,
            gravity_potential_level,
        ]
    )
    east_slope_derivative, north_slope_derivative = extended_slopes(
        joined_state_arrays, face_links, forward_layout
    )
    west_east_wind_after = west_east_wind_part - time_increment * (
        east_slope_derivative[5]
        + east_wind_speed * east_slope_derivative[0]
        + north_wind_speed * north_slope_derivative[0]
    )
    south_north_wind_after = south_north_wind_speed - time_increment * (
        north_slope_derivative[5]
        + east_wind_speed * east_slope_derivative[1]
        + north_wind_speed * north_slope_derivative[1]
    )
    depth_after_update = sheet_depth_state - time_increment * (
        east_slope_derivative[2] + north_slope_derivative[3]
    )
    warmth_after_update = sheet_warmth_state - time_increment * (
        east_wind_speed * east_slope_derivative[4] + north_wind_speed * north_slope_derivative[4]
    )
    zonal_cost = inverse_misfit_variance[0] * west_east_wind_after
    meridional_cost = inverse_misfit_variance[1] * south_north_wind_after
    thickness_cost = inverse_misfit_variance[2] * depth_after_update
    heat_misfit_penalty = inverse_misfit_variance[3] * warmth_after_update
    sensitive = jnp.stack(
        [
            east_wind_speed * zonal_cost,
            east_wind_speed * meridional_cost,
            north_wind_speed * zonal_cost,
            north_wind_speed * meridional_cost,
            zonal_cost,
            meridional_cost,
            thickness_cost,
            east_wind_speed * heat_misfit_penalty,
            north_wind_speed * heat_misfit_penalty,
        ]
    )
    east_slope_derivative, north_slope_derivative = extended_slopes(
        sensitive, face_links, adjoint_layout
    )
    geo_back = time_increment * (east_slope_derivative[4] + north_slope_derivative[5])
    flux_east_back = time_increment * east_slope_derivative[6]
    flux_north_back = time_increment * north_slope_derivative[6]
    zonal_back = (
        zonal_cost
        + time_increment * (east_slope_derivative[0] + north_slope_derivative[2])
        + layer_mass * flux_east_back
    )
    meridional_back = (
        meridional_cost
        + time_increment * (east_slope_derivative[1] + north_slope_derivative[3])
        + layer_mass * flux_north_back
    )
    warmth_back = (
        heat_misfit_penalty
        + time_increment * (east_slope_derivative[7] + north_slope_derivative[8])
        + geo_back
    )
    thickness_back = (
        thickness_cost
        + east_wind_speed * flux_east_back
        + north_wind_speed * flux_north_back
        + load_of(trajectory_heat_factor * geo_back)
    )
    adjoint_out = jnp.stack([zonal_back, meridional_back, thickness_back, warmth_back], axis=1)
    return probes + spread[None] * adjoint_out


def rolled(tile, shift, axis):
    return pltpu.roll(tile, shift % tile.shape[axis], axis)


def gathered(tile, index, axis):
    return jnp.take_along_axis(tile, index, axis=axis, mode="promise_in_bounds")


def tile_kernel(
    count,
    faces,
    probes_hbm,
    wind_hbm,
    mass_hbm,
    heat_hbm,
    spread_hbm,
    variance_hbm,
    links_hbm,
    out_ref,
    probes_ref,
    wind_ref,
    mass_ref,
    heat_ref,
    spread_ref,
    variance_ref,
    links_ref,
    take_sem,
    strips_f,
    strips_a,
    strips_p,
    kept,
    raw,
    coefs,
    turned,
    halo_f,
    halo_a,
    slots_f,
    slots_a,
    ghosts,
    below_ref,
    above_ref,
    column_f,
    column_a,
    rows_f,
    rows_a,
    rows_p,
    row_halo_f,
    row_halo_a,
    row_slots_f,
    row_slots_a,
    send_f,
    send_a,
    recv_halo_f,
    recv_halo_a,
    recv_slot_f,
    recv_slot_a,
    send_rows_f,
    send_rows_a,
    recv_row_halo_f,
    recv_row_halo_a,
    recv_row_slot_f,
    recv_row_slot_a,
    send_below,
    send_above,
    recv_below,
    recv_above,
):
    level = lax.axis_index("face")
    row = lax.axis_index("tx")
    column = lax.axis_index("ty")
    probe_count = probes_ref.shape[0]
    panels = probes_ref.shape[3]
    last = count - 1
    at = [row == 0, row == last, column == 0, column == last]
    on_row = at[0] | at[1]
    on_column = at[2] | at[3]
    corner = on_row & on_column
    middle = (on_row | on_column) & ~corner
    row_edge = jnp.where(at[0], 0, 1)
    column_edge = jnp.where(at[2], 2, 3)
    half = count // 2
    row_part = jnp.where(column < half, 0, 1)
    column_part = jnp.where(row < half, 0, 1)
    row_slot = row_edge * 2 + row_part
    column_slot = column_edge * 2 + column_part
    own_edge = jnp.where(on_row, row_edge, column_edge)
    own_slot = jnp.where(on_row, row_slot, column_slot)
    along = jnp.where(on_row, column, row)
    near = jnp.where(along < half, along, last - along)

    def slot_place(edge, part):
        segment = near if part == 0 else last - near
        return [(0, segment), (last, segment), (segment, 0), (segment, last)][edge]

    beside = [(row - 1, column), (row + 1, column), (row, column - 1), (row, column + 1)]
    corners = [(0, 0), (0, last), (last, 0), (last, last)]

    barrier = pltpu.get_barrier_semaphore()

    def greet(other, place):
        pl.semaphore_signal(
            barrier,
            inc=1,
            device_id={"face": other, "tx": place[0], "ty": place[1]},
            device_id_type=MESH,
        )

    for other in range(faces):
        for d in range(4):
            @pl.when(~at[d])
            def _():
                greet(other, beside[d])

        @pl.when(middle)
        def _():
            for slot in range(8):
                @pl.when((own_slot != slot) | (level != other))
                def _():
                    greet(other, slot_place(slot // 2, slot % 2))

        @pl.when(corner)
        def _():
            for place in corners:
                @pl.when((row != place[0]) | (column != place[1]) | (level != other))
                def _():
                    greet(other, place)

        @pl.when(level != other)
        def _():
            greet(other, (row, column))

    taken = [
        pltpu.make_async_copy(source, target, take_sem.at[i])
        for i, (source, target) in enumerate(
            (
                (probes_hbm, probes_ref),
                (spread_hbm, spread_ref),
                (wind_hbm, wind_ref),
                (mass_hbm, mass_ref),
                (heat_hbm, heat_ref),
                (variance_hbm, variance_ref),
                (links_hbm, links_ref),
            )
        )
    ]
    for copy in taken:
        copy.start()

    expected = (
        faces - 1 + jnp.where(middle, 8 * faces - 1, 0) + jnp.where(corner, 4 * faces - 1, 0)
    )
    for d in range(4):
        expected = expected + jnp.where(at[d], 0, faces)

    sub = lax.broadcasted_iota(jnp.int32, (SUBLANES, LANES), 0)
    lane = lax.broadcasted_iota(jnp.int32, (SUBLANES, LANES), 1)
    inner = lane % SUBLANES
    panel_of = (lane // SUBLANES) % panels
    base = lane - inner
    skew = (inner - sub + SUBLANES) % SUBLANES
    unskew = base + (inner + sub) % SUBLANES

    def packed(tiles):
        width = LANES - SUBLANES * len(tiles)
        return jnp.concatenate(tiles + [jnp.zeros((SUBLANES, width), jnp.float32)], axis=1)

    def per_panel(load):
        return packed([load(f) for f in range(panels)] * probe_count)

    def per_probe(component):
        return packed(
            [
                probes_ref[p, component, 0, f]
                for p in range(probe_count)
                for f in range(panels)
            ]
        )

    def level_copy(other, source, target, send, recv):
        return pltpu.make_async_remote_copy(
            src_ref=source,
            dst_ref=target,
            send_sem=send,
            recv_sem=recv,
            device_id={"face": other},
            device_id_type=MESH,
        )

    def below_copy(other, slot):
        return level_copy(
            other, column_f, below_ref.at[slot], send_below.at[other], recv_below.at[slot]
        )

    def above_copy(other, slot):
        return level_copy(
            other, column_a, above_ref.at[slot], send_above.at[other], recv_above.at[slot]
        )

    nothing = jnp.zeros((SUBLANES, LANES), jnp.float32)

    def columns_of(y_fields):
        low = high = nothing
        for c, field in enumerate(y_fields):
            low = jnp.where(skew == c, gathered(field, base, 1), low)
            high = jnp.where(skew == c, gathered(field, base + (SUBLANES - 1), 1), high)
        return [gathered(gathered(tile, skew, 0), unskew, 1) for tile in (low, high)]

    def write_strips(strips, x_fields, y_fields, first=0):
        low = high = nothing
        for c, field in enumerate(x_fields):
            low = jnp.where(sub == c, field[0:1, :], low)
            high = jnp.where(sub == c, field[SUBLANES - 1 : SUBLANES, :], high)
        tiles = (low, high, *columns_of(y_fields))
        for d, tile in enumerate(tiles):
            strips[d, first : first + SUBLANES] = tile

    def strip_copy(source, target, send, recv, other, place):
        return pltpu.make_async_remote_copy(
            src_ref=source,
            dst_ref=target,
            send_sem=send,
            recv_sem=recv,
            device_id={"face": other, "tx": place[0], "ty": place[1]},
            device_id_type=MESH,
        )

    def send_far(buffers, target=None):
        strips, halo, slots, send, recv_halo, recv_slot = buffers
        across = target is not None
        other = target if across else level
        first_send = 5 * target if across else 0
        first_slot = 8 * level if across else 0
        group = level if across else 0

        @pl.when(middle)
        def _():
            for slot in range(8):
                @pl.when((own_slot != slot) | across)
                def _():
                    strip_copy(
                        strips.at[own_edge],
                        slots.at[first_slot + own_slot],
                        send.at[first_send + 4],
                        recv_slot.at[group],
                        other,
                        slot_place(slot // 2, slot % 2),
                    ).start()

        @pl.when(corner)
        def _():
            for place in corners:
                @pl.when((row != place[0]) | (column != place[1]) | across)
                def _():
                    for edge, slot in ((row_edge, row_slot), (column_edge, column_slot)):
                        strip_copy(
                            strips.at[edge],
                            slots.at[first_slot + slot],
                            send.at[first_send + 4],
                            recv_slot.at[group],
                            other,
                            place,
                        ).start()

    def send_near(buffers, target=None):
        strips, halo, slots, send, recv_halo, recv_slot = buffers
        across = target is not None
        other = target if across else level
        first_send = 5 * target if across else 0
        first_halo = 4 * level if across else 0
        for d in range(4):
            @pl.when(~at[d])
            def _():
                strip_copy(
                    strips.at[d, pl.ds(0, halo.shape[1])],
                    halo.at[first_halo + (d ^ 1)],
                    send.at[first_send + d],
                    recv_halo.at[first_halo + (d ^ 1)],
                    other,
                    beside[d],
                ).start()

    def each_wait(buffers, sent, far, other=None):
        strips, halo, slots, send, recv_halo, recv_slot = buffers
        across = other is not None
        first_send = 5 * other if across else 0
        first_halo = 4 * other if across else 0
        group = other if across else 0

        def ended(ref, send_sem, recv_sem):
            copy = strip_copy(ref, ref, send_sem, recv_sem, level, (row, column))
            if sent:
                copy.wait_send()
            else:
                copy.wait_recv()

        if not far:
            for d in range(4):
                @pl.when(~at[d])
                def _():
                    ended(halo.at[0], send.at[first_send + d], recv_halo.at[first_halo + d])

            return
        for role, number in ((middle, 8 if across else 7), (corner, 8 if across else 6)):
            @pl.when(role)
            def _():
                ended(
                    slots.at[pl.ds(0, number)], send.at[first_send + 4], recv_slot.at[group]
                )

    forward = (strips_f, halo_f, slots_f, send_f, recv_halo_f, recv_slot_f)
    adjoint = (strips_a, halo_a, slots_a, send_a, recv_halo_a, recv_slot_a)
    partial = (strips_p, *adjoint[1:])
    forward_rows = (
        rows_f, row_halo_f, row_slots_f, send_rows_f, recv_row_halo_f, recv_row_slot_f
    )
    adjoint_rows = (
        rows_a, row_halo_a, row_slots_a, send_rows_a, recv_row_halo_a, recv_row_slot_a
    )
    partial_rows = (rows_p, *adjoint_rows[1:])

    def keep_own(strips, slots):
        @pl.when(on_row)
        def _():
            slots[row_slot] = strips[row_edge]

        @pl.when(on_column)
        def _():
            slots[column_slot] = strips[column_edge]

    def with_levels(strip, rows, stride, index, is_adjoint):
        if is_adjoint:
            for other in range(1, faces):
                strip = jnp.where(sub == 4 + other, rows[stride * other + index], strip)
            return strip
        beneath = jnp.zeros((1, LANES), jnp.float32)
        for other in range(faces - 1):
            beneath = beneath + jnp.where(level > other, rows[stride * other + index], 0.0)
        return strip + jnp.where(sub == 4, rolled(strip, -1, 0) * beneath, 0.0)

    for copy in taken[:2]:
        copy.wait()
    probe_h = per_probe(2)
    spread_h = per_panel(lambda f: spread_ref[2, 0, f])
    h = spread_h * probe_h
    column_f[...] = h
    rows_f[0] = h[0:1, :]
    rows_f[1] = h[SUBLANES - 1 : SUBLANES, :]
    low, high = columns_of((h,))
    rows_f[2] = low[0:1, :]
    rows_f[3] = high[0:1, :]
    probe_z, probe_m, probe_t = per_probe(0), per_probe(1), per_probe(3)
    spread_z, spread_m, spread_t = [
        per_panel(lambda f, c=c: spread_ref[c, 0, f]) for c in (0, 1, 3)
    ]
    for copy in taken[2:]:
        copy.wait()
    u, v = [per_panel(lambda f, c=c: wind_ref[c, 0, f]) for c in range(2)]
    mass = per_panel(lambda f: mass_ref[0, f])
    heat = per_panel(lambda f: heat_ref[0, f])
    var_z, var_m, var_h, var_t = [
        per_panel(lambda f, c=c: variance_ref[c, 0, f]) for c in range(4)
    ]
    z, m, t = spread_z * probe_z, spread_m * probe_m, spread_t * probe_t
    fx = u * h + mass * z
    fy = v * h + mass * m

    def links_of(edge, part, is_row):
        zero = jnp.zeros((SUBLANES, LANES), jnp.int32)
        source = flip = slot = normal = tangent = zero
        for f in range(panels):
            here = panel_of == f
            entries = [links_ref[f, edge, 3 + i] for i in range(4)]
            first, second = entries[0] + entries[1], entries[2] + entries[3]
            turned = links_ref[f, edge, 2]
            held = links_ref[f, edge, 1] * 2 + jnp.where(turned == 1, 1 - part, part)
            source = jnp.where(here, links_ref[f, edge, 0], source)
            flip = jnp.where(here, turned, flip)
            slot = jnp.where(here, held, slot)
            normal = jnp.where(here, first if is_row else second, normal)
            tangent = jnp.where(here, second if is_row else first, tangent)
        shifted = base + SUBLANES * (source - panel_of)

        def index_of(along):
            index = shifted + jnp.where(flip == 1, SUBLANES - 1 - along, along)
            return jnp.where(lane < SUBLANES * panels * probe_count, index, lane)

        straight = index_of(inner)
        index = straight if is_row else index_of(skew)
        normal, tangent = normal.astype(jnp.float32), tangent.astype(jnp.float32)
        wind = jnp.where(sub == 0, normal, jnp.where(sub == 1, tangent, 1.0))
        ahead = jnp.where(sub == 2, normal, jnp.where(sub == 6, tangent, wind))
        back = jnp.where(
            sub == 1, normal * tangent, jnp.where((sub == 0) | (sub == 3), 1.0, normal)
        )
        return index, slot, ahead, back, straight, wind

    def ghost_across(slots, row_slots, links, is_adjoint, straight=False):
        slot = links[1]
        index = links[4] if straight else links[0]
        strip = nothing
        for number in range(8):
            held = slots[number, 0:SUBLANES]
            held = with_levels(held, row_slots, 8, number, is_adjoint)
            strip = jnp.where(slot == number, gathered(held, index, 1), strip)
        return strip * (links[3] if is_adjoint else links[2])

    def coefs_across(links):
        strip = nothing
        for number in range(8):
            held = slots_f[number, SUBLANES : 2 * SUBLANES]
            strip = jnp.where(links[1] == number, gathered(held, links[4], 1), strip)
        return strip * links[5]

    def ghosts_near(buffers, rows_buffers, is_adjoint):
        halo, row_halo = buffers[1], rows_buffers[1]
        for d in range(4):
            @pl.when(~at[d])
            def _():
                strip = with_levels(halo[d], row_halo, 4, d, is_adjoint)
                ghosts[d] = strip if d < 2 else gathered(strip, base + skew, 1)

    def ghosts_far(row_tile, column_tile):
        @pl.when(on_row)
        def _():
            ghosts[row_edge] = row_tile()

        @pl.when(on_column)
        def _():
            ghosts[column_edge] = column_tile()

    def correct(side, parts):
        normal, tangent, depth, warmth = parts
        wind = coefs[side, 0:1]
        rows = (wind * normal, wind * tangent, normal, depth, wind * warmth)
        for c, value in enumerate(rows):
            kept[side, c : c + 1] = kept[side, c : c + 1] + value

    def correct_across(side, edge, low):
        half_step = jnp.where(low, -0.5 * time_increment, 0.5 * time_increment)
        wind, _, var_n, var_s, var_d, var_w = [coefs[side, c : c + 1] for c in range(6)]
        normal, tangent, flux, warmth = [strips_f[edge, c : c + 1] for c in range(4)]
        potential = strips_p[edge, 5:6]
        parts = (
            var_n * (potential + wind * normal),
            var_s * (wind * tangent),
            var_d * flux,
            var_w * (wind * warmth),
        )
        correct(side, [half_step * part for part in parts])

    def correct_corner(side, low, end, far_end):
        turned[side] = gathered(raw[1 - side], base + far_end, 1)
        sign = jnp.where(at[0] == at[2], 1.0, -1.0)
        half_step = jnp.where(low, 0.5 * time_increment, -0.5 * time_increment)
        side_wind, var_n, var_s, var_d, var_w = [coefs[side, c : c + 1] for c in range(1, 6)]
        normal = sign * turned[side, 0:1]
        tangent = -sign * turned[side, 1:2]
        flux = -sign * turned[side, 6:7]
        warmth, potential = turned[side, 3:4], turned[side, 4:5]
        parts = (
            var_n * (side_wind * normal),
            var_s * (potential + side_wind * tangent),
            var_d * flux,
            var_w * (side_wind * warmth),
        )
        here = inner[0:1] == end
        correct(side, [jnp.where(here, half_step * part, 0.0) for part in parts])

    def slopes_of(x_fields, y_fields):
        low, high = ghosts[0], ghosts[1]
        east = []
        for c, field in enumerate(x_fields):
            before = jnp.where(sub == 0, low[c : c + 1, :], rolled(field, 1, 0))
            after = jnp.where(sub == SUBLANES - 1, high[c : c + 1, :], rolled(field, -1, 0))
            east.append(0.5 * (after - before))
        low, high = gathered(ghosts[2], skew, 0), gathered(ghosts[3], skew, 0)
        north = []
        for c, field in enumerate(y_fields):
            place = base + (sub + c) % SUBLANES
            before = jnp.where(inner == 0, gathered(low, place, 1), rolled(field, 1, 1))
            after = jnp.where(
                inner == SUBLANES - 1, gathered(high, place, 1), rolled(field, -1, 1)
            )
            north.append(0.5 * (after - before))
        return east, north

    geo = t + heat * h
    write_strips(strips_f, (z, m, fx, t, geo, heat, fy), (m, z, fy, t, geo, heat, fx))
    write_strips(
        strips_f,
        (u, v, var_z, var_m, var_h, var_t),
        (v, u, var_m, var_z, var_h, var_t),
        SUBLANES,
    )
    pl.semaphore_wait(barrier, expected)
    for other in range(1, faces):
        @pl.when(level < other)
        def _():
            below_copy(other, level).start()
            send_near(forward_rows, other)
    send_near(forward)
    for other in range(1, faces):
        @pl.when(level < other)
        def _():
            send_far(forward_rows, other)
    send_far(forward)

    keep_own(strips_f, slots_f)
    kept[...] = jnp.zeros_like(kept)
    row_links = links_of(row_edge, row_part, True)
    column_links = links_of(column_edge, column_part, False)

    def image_of():
        east, north = slopes_of((z, m, fx, t, geo), (m, z, fy, t, geo))
        zc = var_z * (z - time_increment * (east[4] + u * east[0] + v * north[1]))
        mc = var_m * (m - time_increment * (north[4] + u * east[1] + v * north[0]))
        hc = var_h * (h - time_increment * (east[2] + north[2]))
        tc = var_t * (t - time_increment * (u * east[3] + v * north[3]))
        x_fields = (u * zc, u * mc, zc, hc, u * tc)
        y_fields = (v * mc, v * zc, mc, hc, v * tc)
        return zc, mc, hc, tc, x_fields, y_fields

    each_wait(forward, False, False)
    for other in range(faces - 1):
        @pl.when(level > other)
        def _():
            below_copy(other, other).wait_recv()
            each_wait(forward_rows, False, False, other)

    for other in range(faces - 1):
        geo = geo + heat * jnp.where(level > other, below_ref[other], 0.0)
    ghosts_near(forward, forward_rows, False)
    ghosts_far(lambda: nothing, lambda: nothing)
    x_fields, y_fields = image_of()[4:]
    write_strips(strips_p, x_fields + (geo,), y_fields + (geo,))
    for d in range(4):
        rows_p[d] = strips_p[d][2:3, :]
    for other in range(faces):
        @pl.when(level > other)
        def _():
            send_far(partial_rows, other)
    send_far(partial)
    keep_own(strips_p, slots_a)

    each_wait(forward, False, True)
    for other in range(faces - 1):
        @pl.when(level > other)
        def _():
            each_wait(forward_rows, False, True, other)

    ghosts_far(
        lambda: ghost_across(slots_f, row_slots_f, row_links, False),
        lambda: ghost_across(slots_f, row_slots_f, column_links, False),
    )
    zc, mc, hc, tc, x_fields, y_fields = image_of()
    write_strips(strips_a, x_fields, y_fields)
    for d in range(4):
        rows_a[d] = strips_a[d][2:3, :]
    for other in range(faces):
        @pl.when(level > other)
        def _():
            send_near(adjoint_rows, other)
    send_near(adjoint)

    @pl.when(on_row)
    def _():
        coefs[0] = coefs_across(row_links)
        correct_across(0, row_edge, at[0])

    @pl.when(on_column)
    def _():
        coefs[1] = coefs_across(column_links)
        correct_across(1, column_edge, at[2])

    @pl.when(corner)
    def _():
        raw[0] = ghosts[row_edge]
        raw[1] = ghost_across(slots_f, row_slots_f, column_links, False, True)
        row_end = jnp.where(at[0], 0, SUBLANES - 1)
        column_end = jnp.where(at[2], 0, SUBLANES - 1)
        correct_corner(0, at[2], column_end, row_end)
        correct_corner(1, at[0], row_end, column_end)

    column_a[0], column_a[1], column_a[2] = zc, mc, heat
    column_a[3] = jnp.where(sub == 0, kept[0, 2:3], kept[1, 2:3])
    for other in range(faces):
        @pl.when(level > other)
        def _():
            above_copy(other, level).start()

    for far in (False, True):
        each_wait(forward, True, far)
        each_wait(partial if far else adjoint, True, far)
    for other in range(faces):
        @pl.when(level < other)
        def _():
            below_copy(other, level).wait_send()
            for far in (False, True):
                each_wait(forward_rows, True, far, other)

        @pl.when(level > other)
        def _():
            above_copy(other, level).wait_send()
            for far in (False, True):
                each_wait(adjoint_rows, True, far, other)

    each_wait(adjoint, False, False)
    each_wait(adjoint, False, True)
    for other in range(1, faces):
        @pl.when(level < other)
        def _():
            above_copy(other, other).wait_recv()
            each_wait(adjoint_rows, False, False, other)
            each_wait(adjoint_rows, False, True, other)

    def correction(side):
        tile = kept[side]
        for other in range(1, faces):
            upper = above_ref[other, 3, side : side + 1]
            tile = jnp.where((sub == 4 + other) & (level < other), upper, tile)
        return tile

    ghosts_near(adjoint, adjoint_rows, True)
    ghosts_far(
        lambda: ghost_across(slots_a, row_slots_a, row_links, True) + correction(0),
        lambda: ghost_across(slots_a, row_slots_a, column_links, True)
        + gathered(correction(1), base + skew, 1),
    )
    above = [above_ref[other] for other in range(1, faces)]
    east, north = slopes_of(
        x_fields + tuple(tiles[0] for tiles in above),
        y_fields + tuple(tiles[1] for tiles in above),
    )
    geo_back = time_increment * (east[2] + north[2])
    load = heat * geo_back
    for other, tiles in enumerate(above, 1):
        upper = tiles[2] * (time_increment * (east[4 + other] + north[4 + other]))
        load = load + jnp.where(level < other, upper, 0.0)

    flux_east = time_increment * east[3]
    flux_north = time_increment * north[3]
    z_back = zc + time_increment * (east[0] + north[1]) + mass * flux_east
    m_back = mc + time_increment * (east[1] + north[0]) + mass * flux_north
    t_back = tc + time_increment * (east[4] + north[4]) + geo_back
    h_back = hc + u * flux_east + v * flux_north + load
    out_ref[0] = probe_z + spread_z * z_back
    out_ref[1] = probe_m + spread_m * m_back
    out_ref[2] = probe_h + spread_h * h_back
    out_ref[3] = probe_t + spread_t * t_back


def unpack_kernel(packed_ref, out_ref):
    probe_count, components, _, panels, _, _ = out_ref.shape
    for component in range(components):
        tile = packed_ref[component]
        for p in range(probe_count):
            for f in range(panels):
                start = (p * panels + f) * SUBLANES
                out_ref[p, component, 0, f] = tile[:, start : start + SUBLANES]


def fused(count, faces, *operands):
    tile = (SUBLANES, LANES)
    vmem = pl.BlockSpec(memory_space=pltpu.VMEM)
    whole = pl.BlockSpec(memory_space=pl.ANY)
    probes = operands[0]
    strips = pltpu.VMEM((4, *tile), jnp.float32)
    slots = pltpu.VMEM((8, *tile), jnp.float32)

    def edge_rows(number):
        return pltpu.VMEM((number, 1, LANES), jnp.float32)

    dma = pltpu.SemaphoreType.DMA
    packed = pl.pallas_call(
        functools.partial(tile_kernel, count, faces),
        out_shape=pltpu.VMEM((probes.shape[1], *tile), probes.dtype),
        in_specs=[whole] * len(operands),
        out_specs=vmem,
        scratch_shapes=[pltpu.VMEM(x.shape, x.dtype) for x in operands[:-1]]
        + [
            pltpu.SMEM(operands[-1].shape, operands[-1].dtype),
            dma((len(operands),)),
        ]
        + [pltpu.VMEM((4, 2 * SUBLANES, LANES), jnp.float32), strips, strips]
        + [pltpu.VMEM((2, *tile), jnp.float32)] * 4
        + [strips] * 2
        + [pltpu.VMEM((8, 2 * SUBLANES, LANES), jnp.float32), slots]
        + [strips]
        + [pltpu.VMEM((faces, *tile), jnp.float32), pltpu.VMEM((faces, 4, *tile), jnp.float32)]
        + [pltpu.VMEM(tile, jnp.float32), pltpu.VMEM((4, *tile), jnp.float32)]
        + [edge_rows(4)] * 3
        + [edge_rows(4 * faces)] * 2
        + [edge_rows(8 * faces)] * 2
        + [dma((5,))] * 2
        + [dma((4,))] * 2
        + [dma((1,))] * 2
        + [dma((5 * faces,))] * 2
        + [dma((4 * faces,))] * 2
        + [dma((faces,))] * 2
        + [dma((faces,))] * 4,
        compiler_params=pltpu.CompilerParams(collective_id=0, has_side_effects=True),
    )(*operands)
    return pl.pallas_call(
        unpack_kernel,
        out_shape=jax.ShapeDtypeStruct(probes.shape, probes.dtype),
        in_specs=[vmem],
        out_specs=vmem,
        compiler_params=pltpu.CompilerParams(vmem_limit_bytes=VMEM_BYTES),
    )(packed)


def solution(mesh):
    count, faces = mesh.shape["tx"], mesh.shape["face"]

    def chosen(*operands):
        probe_count, _, levels, panels, rows, columns = operands[0].shape
        fits = (
            levels == 1
            and count == mesh.shape["ty"]
            and count % 2 == 0
            and rows == columns == SUBLANES
            and faces + 4 <= SUBLANES
            and probe_count * panels * SUBLANES < LANES
        )
        return fused(count, faces, *operands) if fits else body(*operands)

    return jax.shard_map(
        chosen,
        mesh=mesh,
        in_specs=(
            P(None, None, "face", None, "tx", "ty"),
            P(None, "face", None, "tx", "ty"),
            P("face", None, "tx", "ty"),
            P("face", None, "tx", "ty"),
            P(None, "face", None, "tx", "ty"),
            P(None, "face", None, "tx", "ty"),
            P(),
        ),
        out_specs=P(None, None, "face", None, "tx", "ty"),
        check_vma=False,
    )
```

```python
import functools

import jax
import jax.numpy as jnp
from jax import lax
from jax.experimental import pallas as pl
from jax.experimental.pallas import tpu as pltpu
from jax.sharding import PartitionSpec as P

MESH = pl.DeviceIdType.MESH
SUBLANES = 8
LANES = 128
VMEM_BYTES = 4 * 2**20

time_increment = 0.3
forward_layout = (("vector", 0), ("vector", 2), ("scalar", 4), ("scalar", 5))
adjoint_layout = (("tensor", 0), ("vector", 4), ("scalar", 6), ("vector", 7))


def padded_2(array, sides, width):
    for axis, dim in sides:
        devices, length = (lax.axis_size(axis), array.shape[dim])
        up = [(i, (i + 1) % devices) for i in range(devices - 1)]
        down = [(j, i) for i, j in up]
        last = lax.slice_in_dim(array, length - width, length, axis=dim)
        leading = lax.slice_in_dim(array, 0, width, axis=dim)
        before = lax.ppermute(last, axis, up)
        after = lax.ppermute(leading, axis, down)
        array = jnp.concatenate([before, array, after], axis=dim)
    return array


def carried_in(value, axis, join, neutral, backward):
    count, mine = (lax.axis_size(axis), lax.axis_index(axis))
    pieces = lax.all_gather(value, axis)
    if backward:
        pieces = pieces[::-1]
        mine = count - 1 - mine
    total = jnp.full_like(value, 0) + jnp.asarray(neutral, value.dtype)

    def hop(position, total):
        longer = join(total, pieces[position])
        return jnp.where(position < mine, longer, total)

    return lax.fori_loop(0, count - 1, hop, total)


def carry_pair(leading, trailing, entries):
    return (
        entries[0] * leading + entries[1] * trailing,
        entries[2] * leading + entries[3] * trailing,
    )


def rotate_edge(edge_strip, matrix_codes, layout):
    matrix = matrix_codes.astype(edge_strip.dtype)
    entries = [matrix[:, column].reshape(1, 1, 6, 1) for column in range(4)]
    channels = [edge_strip[number] for number in range(edge_strip.shape[0])]
    for species, offset in layout:
        if species == "vector":
            channels[offset], channels[offset + 1] = carry_pair(
                channels[offset], channels[offset + 1], entries
            )
        elif species == "tensor":
            channels[offset], channels[offset + 1] = carry_pair(
                channels[offset], channels[offset + 1], entries
            )
            channels[offset + 2], channels[offset + 3] = carry_pair(
                channels[offset + 2], channels[offset + 3], entries
            )
            channels[offset], channels[offset + 2] = carry_pair(
                channels[offset], channels[offset + 2], entries
            )
            channels[offset + 1], channels[offset + 3] = carry_pair(
                channels[offset + 1], channels[offset + 3], entries
            )
    return jnp.stack(channels)


def orient(edge_rows, face_links, side, layout):
    lines = edge_rows.reshape(edge_rows.shape[:3] + (-1, edge_rows.shape[5]))
    sides = edge_rows.shape[4]
    chosen = jnp.concatenate(
        [
            lax.dynamic_slice_in_dim(
                lines, face_links[f, side, 0] * sides + face_links[f, side, 1], 1, 3
            )
            for f in range(face_links.shape[0])
        ],
        axis=3,
    )
    flipped = (face_links[:, side, 2] == 1).reshape(1, 1, 1, 6, 1)
    chosen = jnp.where(flipped, chosen[..., ::-1], chosen)
    return rotate_edge(chosen, face_links[:, side, 3:7], layout)


def face_rows(fields):
    tile_row = lax.axis_index("tx")
    tile_column = lax.axis_index("ty")
    low_rows = jnp.where(tile_row == 0, fields[..., 0, :], 0.0)
    high_rows = jnp.where(tile_row == lax.axis_size("tx") - 1, fields[..., -1, :], 0.0)
    low_columns = jnp.where(tile_column == 0, fields[..., :, 0], 0.0)
    high_columns = jnp.where(tile_column == lax.axis_size("ty") - 1, fields[..., :, -1], 0.0)
    row_pair = jnp.stack([low_rows, high_rows], axis=4)
    column_pair = jnp.stack([low_columns, high_columns], axis=4)
    row_full = lax.psum(lax.all_gather(row_pair, "ty", axis=5, tiled=True), "tx")
    column_full = lax.psum(lax.all_gather(column_pair, "tx", axis=5, tiled=True), "ty")
    return jnp.concatenate([row_full, column_full], axis=4)


def extended_slopes(fields, face_links, layout):
    row_cells = fields.shape[4]
    column_cells = fields.shape[5]
    tile_row = lax.axis_index("tx")
    tile_column = lax.axis_index("ty")
    padded = padded_2(fields, (("tx", 4), ("ty", 5)), 1)
    edge_rows = face_rows(fields)
    western = lax.dynamic_slice_in_dim(
        orient(edge_rows, face_links, 0, layout), tile_column * column_cells, column_cells, 4
    )
    eastern = lax.dynamic_slice_in_dim(
        orient(edge_rows, face_links, 1, layout), tile_column * column_cells, column_cells, 4
    )
    southern = lax.dynamic_slice_in_dim(
        orient(edge_rows, face_links, 2, layout), tile_row * row_cells, row_cells, 4
    )
    northern = lax.dynamic_slice_in_dim(
        orient(edge_rows, face_links, 3, layout), tile_row * row_cells, row_cells, 4
    )
    row_number = lax.broadcasted_iota(jnp.int32, (row_cells, column_cells), 0)
    column_number = lax.broadcasted_iota(jnp.int32, (row_cells, column_cells), 1)
    first_row = (row_number == 0) & (tile_row == 0)
    last_row = (row_number == row_cells - 1) & (tile_row == lax.axis_size("tx") - 1)
    first_column = (column_number == 0) & (tile_column == 0)
    last_column = (column_number == column_cells - 1) & (tile_column == lax.axis_size("ty") - 1)
    east_slope_derivative = 0.5 * (padded[..., 2:, 1:-1] - padded[..., :-2, 1:-1])
    east_slope_derivative = (
        east_slope_derivative
        + jnp.where(last_row, 0.5 * eastern[..., None, :], 0.0)
        - jnp.where(first_row, 0.5 * western[..., None, :], 0.0)
    )
    north_slope_derivative = 0.5 * (padded[..., 1:-1, 2:] - padded[..., 1:-1, :-2])
    north_slope_derivative = (
        north_slope_derivative
        + jnp.where(last_column, 0.5 * northern[..., :, None], 0.0)
        - jnp.where(first_column, 0.5 * southern[..., :, None], 0.0)
    )
    return (east_slope_derivative, north_slope_derivative)


def pressure_of(sheet_depth_state):
    within = jnp.cumsum(sheet_depth_state, axis=1)
    totals_here = within[:, -1]
    underneath = carried_in(totals_here, "face", jnp.add, jnp.zeros_like(totals_here), False)
    return within + underneath[:, None]


def load_of(sensitivity):
    within = jnp.flip(jnp.cumsum(jnp.flip(sensitivity, 1), axis=1), 1)
    totals_here = within[:, 0]
    overhead = carried_in(totals_here, "face", jnp.add, jnp.zeros_like(totals_here), True)
    return within + overhead[:, None]


def body(
    probes,
    background_wind,
    layer_mass,
    trajectory_heat_factor,
    spread,
    inverse_misfit_variance,
    face_links,
):
    normalised_state_array = spread[None] * probes
    west_east_wind_part, south_north_wind_speed, sheet_depth_state, sheet_warmth_state = (
        normalised_state_array[:, 0],
        normalised_state_array[:, 1],
        normalised_state_array[:, 2],
        normalised_state_array[:, 3],
    )
    east_wind_speed, north_wind_speed = (background_wind[0], background_wind[1])
    ground_barometric_load = pressure_of(sheet_depth_state)
    gravity_potential_level = sheet_warmth_state + trajectory_heat_factor * ground_barometric_load
    east_mass_transport = east_wind_speed * sheet_depth_state + layer_mass * west_east_wind_part
    north_mass_transport = (
        north_wind_speed * sheet_depth_state + layer_mass * south_north_wind_speed
    )
    joined_state_arrays = jnp.stack(
        [
            west_east_wind_part,
            south_north_wind_speed,
            east_mass_transport,
            north_mass_transport,
            sheet_warmth_state,
            gravity_potential_level,
        ]
    )
    east_slope_derivative, north_slope_derivative = extended_slopes(
        joined_state_arrays, face_links, forward_layout
    )
    west_east_wind_after = west_east_wind_part - time_increment * (
        east_slope_derivative[5]
        + east_wind_speed * east_slope_derivative[0]
        + north_wind_speed * north_slope_derivative[0]
    )
    south_north_wind_after = south_north_wind_speed - time_increment * (
        north_slope_derivative[5]
        + east_wind_speed * east_slope_derivative[1]
        + north_wind_speed * north_slope_derivative[1]
    )
    depth_after_update = sheet_depth_state - time_increment * (
        east_slope_derivative[2] + north_slope_derivative[3]
    )
    warmth_after_update = sheet_warmth_state - time_increment * (
        east_wind_speed * east_slope_derivative[4] + north_wind_speed * north_slope_derivative[4]
    )
    zonal_cost = inverse_misfit_variance[0] * west_east_wind_after
    meridional_cost = inverse_misfit_variance[1] * south_north_wind_after
    thickness_cost = inverse_misfit_variance[2] * depth_after_update
    heat_misfit_penalty = inverse_misfit_variance[3] * warmth_after_update
    sensitive = jnp.stack(
        [
            east_wind_speed * zonal_cost,
            east_wind_speed * meridional_cost,
            north_wind_speed * zonal_cost,
            north_wind_speed * meridional_cost,
            zonal_cost,
            meridional_cost,
            thickness_cost,
            east_wind_speed * heat_misfit_penalty,
            north_wind_speed * heat_misfit_penalty,
        ]
    )
    east_slope_derivative, north_slope_derivative = extended_slopes(
        sensitive, face_links, adjoint_layout
    )
    geo_back = time_increment * (east_slope_derivative[4] + north_slope_derivative[5])
    flux_east_back = time_increment * east_slope_derivative[6]
    flux_north_back = time_increment * north_slope_derivative[6]
    zonal_back = (
        zonal_cost
        + time_increment * (east_slope_derivative[0] + north_slope_derivative[2])
        + layer_mass * flux_east_back
    )
    meridional_back = (
        meridional_cost
        + time_increment * (east_slope_derivative[1] + north_slope_derivative[3])
        + layer_mass * flux_north_back
    )
    warmth_back = (
        heat_misfit_penalty
        + time_increment * (east_slope_derivative[7] + north_slope_derivative[8])
        + geo_back
    )
    thickness_back = (
        thickness_cost
        + east_wind_speed * flux_east_back
        + north_wind_speed * flux_north_back
        + load_of(trajectory_heat_factor * geo_back)
    )
    adjoint_out = jnp.stack([zonal_back, meridional_back, thickness_back, warmth_back], axis=1)
    return probes + spread[None] * adjoint_out


def rolled(tile, shift, axis):
    return pltpu.roll(tile, shift % tile.shape[axis], axis)


def gathered(tile, index, axis):
    return jnp.take_along_axis(tile, index, axis=axis, mode="promise_in_bounds")


def tile_kernel(
    count,
    faces,
    probes_hbm,
    wind_hbm,
    mass_hbm,
    heat_hbm,
    spread_hbm,
    variance_hbm,
    links_hbm,
    out_ref,
    probes_ref,
    wind_ref,
    mass_ref,
    heat_ref,
    spread_ref,
    variance_ref,
    links_ref,
    take_sem,
    strips_f,
    strips_a,
    strips_p,
    kept,
    kept_ref,
    coefs,
    turned,
    halo_f,
    halo_a,
    slots_f,
    slots_a,
    below_ref,
    above_ref,
    column_f,
    column_a,
    rows_f,
    rows_a,
    rows_p,
    far_f,
    far_p,
    far_rows_f,
    far_rows_p,
    row_halo_f,
    row_halo_a,
    row_slots_f,
    row_slots_a,
    send_f,
    send_a,
    recv_halo_f,
    recv_halo_a,
    recv_slot_f,
    recv_slot_a,
    send_rows_f,
    send_rows_a,
    recv_row_halo_f,
    recv_row_halo_a,
    recv_row_slot_f,
    recv_row_slot_a,
    send_below,
    send_above,
    recv_below,
    recv_above,
    send_kept,
    recv_kept,
):
    level = lax.axis_index("face")
    row = lax.axis_index("tx")
    column = lax.axis_index("ty")
    probe_count = probes_ref.shape[0]
    panels = probes_ref.shape[3]
    last = count - 1
    at = [row == 0, row == last, column == 0, column == last]
    on_row = at[0] | at[1]
    on_column = at[2] | at[3]
    corner = on_row & on_column
    middle = (on_row | on_column) & ~corner
    row_edge = jnp.where(at[0], 0, 1)
    column_edge = jnp.where(at[2], 2, 3)
    half = count // 2
    row_part = jnp.where(column < half, 0, 1)
    column_part = jnp.where(row < half, 0, 1)
    row_slot = row_edge * 2 + row_part
    column_slot = column_edge * 2 + column_part
    own_edge = jnp.where(on_row, row_edge, column_edge)
    own_slot = jnp.where(on_row, row_slot, column_slot)
    along = jnp.where(on_row, column, row)
    near = jnp.where(along < half, along, last - along)

    def slot_place(slot):
        edge, part = slot // 2, slot % 2
        segment = near + part * (last - 2 * near)
        return (
            jnp.where(edge < 2, edge * last, segment),
            jnp.where(edge < 2, segment, (edge - 2) * last),
        )

    own_corner = row_edge * 2 + column_edge - 2

    def corner_place(number):
        return (number // 2 * last, number % 2 * last)

    beside = [(row - 1, column), (row + 1, column), (row, column - 1), (row, column + 1)]

    barrier = pltpu.get_barrier_semaphore()

    def greet(other, place):
        pl.semaphore_signal(
            barrier,
            inc=1,
            device_id={"face": other, "tx": place[0], "ty": place[1]},
            device_id_type=MESH,
        )

    taken = [
        pltpu.make_async_copy(source, target, take_sem.at[i])
        for i, (source, target) in enumerate(
            (
                (probes_hbm, probes_ref),
                (spread_hbm, spread_ref),
                (wind_hbm, wind_ref),
                (mass_hbm, mass_ref),
                (heat_hbm, heat_ref),
                (variance_hbm, variance_ref),
                (links_hbm, links_ref),
            )
        )
    ]
    for copy in taken:
        copy.start()

    @pl.when(middle)
    def _():
        for step in range(1, faces):
            for slot in range(8):
                greet((level + step) % faces, slot_place(slot))
        for step in range(1, 8):
            greet(level, slot_place((own_slot + step) % 8))

    @pl.when(corner)
    def _():
        for step in range(1, faces):
            for number in range(4):
                greet((level + step) % faces, corner_place(number))
        for step in range(1, 4):
            greet(level, corner_place((own_corner + step) % 4))

    for d in range(4):
        @pl.when(~at[d])
        def _():
            for other in range(faces):
                greet(other, beside[d])

    for step in range(1, faces):
        greet((level + step) % faces, (row, column))

    expected = (
        faces - 1 + jnp.where(middle, 8 * faces - 1, 0) + jnp.where(corner, 4 * faces - 1, 0)
    )
    for d in range(4):
        expected = expected + jnp.where(at[d], 0, faces)

    sub = lax.broadcasted_iota(jnp.int32, (SUBLANES, LANES), 0)
    lane = lax.broadcasted_iota(jnp.int32, (SUBLANES, LANES), 1)
    inner = lane % SUBLANES
    panel_of = (lane // SUBLANES) % panels
    base = lane - inner
    skew = (inner - sub + SUBLANES) % SUBLANES
    unskew = base + (inner + sub) % SUBLANES

    def packed(tiles):
        width = LANES - SUBLANES * len(tiles)
        return jnp.concatenate(tiles + [jnp.zeros((SUBLANES, width), jnp.float32)], axis=1)

    def per_panel(load):
        return packed([load(f) for f in range(panels)] * probe_count)

    def per_probe(component):
        return packed(
            [
                probes_ref[p, component, 0, f]
                for p in range(probe_count)
                for f in range(panels)
            ]
        )

    def level_copy(other, source, target, send, recv):
        return pltpu.make_async_remote_copy(
            src_ref=source,
            dst_ref=target,
            send_sem=send,
            recv_sem=recv,
            device_id={"face": other},
            device_id_type=MESH,
        )

    def below_copy(other, slot):
        return level_copy(
            other, column_f, below_ref.at[slot], send_below.at[other], recv_below.at[slot]
        )

    def above_copy(other, slot):
        return level_copy(
            other, column_a, above_ref.at[slot], send_above.at[other], recv_above.at[slot]
        )

    def kept_copy(other, slot):
        return level_copy(
            other, kept, kept_ref.at[slot], send_kept.at[other], recv_kept.at[slot]
        )

    nothing = jnp.zeros((SUBLANES, LANES), jnp.float32)

    def columns_of(y_fields):
        low = high = nothing
        for c, field in enumerate(y_fields):
            low = jnp.where(skew == c, gathered(field, base, 1), low)
            high = jnp.where(skew == c, gathered(field, base + (SUBLANES - 1), 1), high)
        return [gathered(gathered(tile, skew, 0), unskew, 1) for tile in (low, high)]

    def write_strips(strips, x_fields, y_fields, first=0):
        low = high = nothing
        for c, field in enumerate(x_fields):
            low = jnp.where(sub == c, field[0:1, :], low)
            high = jnp.where(sub == c, field[SUBLANES - 1 : SUBLANES, :], high)
        tiles = (low, high, *columns_of(y_fields))
        for d, tile in enumerate(tiles):
            strips[d, first : first + SUBLANES] = tile

    def strip_copy(source, target, send, recv, other, place):
        return pltpu.make_async_remote_copy(
            src_ref=source,
            dst_ref=target,
            send_sem=send,
            recv_sem=recv,
            device_id={"face": other, "tx": place[0], "ty": place[1]},
            device_id_type=MESH,
        )

    def send_far(buffers, target=None):
        strips, halo, slots, send_sem, recv_halo, recv_slot = buffers
        across = target is not None
        other = target if across else level
        first_send = 5 * target if across else 0
        first_slot = 8 * level if across else 0
        group = level if across else 0

        outgoing = outgoings[id(strips)]

        def send(number, slot, place):
            strip_copy(
                outgoing.at[pl.ds(0, number)],
                slots.at[pl.ds(first_slot + slot, number)],
                send_sem.at[first_send + 4],
                recv_slot.at[group],
                other,
                place,
            ).start()

        @pl.when(middle)
        def _():
            for step in range(0 if across else 1, 8):
                send(1, own_slot, slot_place((own_slot + step) % 8))

        @pl.when(corner)
        def _():
            for step in range(0 if across else 1, 4):
                send(2, 2 * own_corner, corner_place((own_corner + step) % 4))

    def send_near(buffers, target=None):
        strips, halo, slots, send, recv_halo, recv_slot = buffers
        across = target is not None
        other = target if across else level
        first_send = 5 * target if across else 0
        first_halo = 4 * level if across else 0
        for d in range(4):
            @pl.when(~at[d])
            def _():
                strip_copy(
                    strips.at[d, pl.ds(0, halo.shape[1])],
                    halo.at[first_halo + (d ^ 1)],
                    send.at[first_send + d],
                    recv_halo.at[first_halo + (d ^ 1)],
                    other,
                    beside[d],
                ).start()

    def each_wait(buffers, sent, far, other=None):
        strips, halo, slots, send, recv_halo, recv_slot = buffers
        across = other is not None
        first_send = 5 * other if across else 0
        first_halo = 4 * other if across else 0
        group = other if across else 0

        def ended(ref, send_sem, recv_sem):
            copy = strip_copy(ref, ref, send_sem, recv_sem, level, (row, column))
            if sent:
                copy.wait_send()
            else:
                copy.wait_recv()

        if not far:
            for d in range(4):
                @pl.when(~at[d])
                def _():
                    ended(halo.at[0], send.at[first_send + d], recv_halo.at[first_halo + d])

            return
        for role, number in ((middle, 8 if across else 7), (corner, 8 if across else 6)):
            @pl.when(role)
            def _():
                ended(
                    slots.at[pl.ds(0, number)], send.at[first_send + 4], recv_slot.at[group]
                )

    forward = (strips_f, halo_f, slots_f, send_f, recv_halo_f, recv_slot_f)
    adjoint = (strips_a, halo_a, slots_a, send_a, recv_halo_a, recv_slot_a)
    partial = (strips_p, *adjoint[1:])
    forward_rows = (
        rows_f, row_halo_f, row_slots_f, send_rows_f, recv_row_halo_f, recv_row_slot_f
    )
    adjoint_rows = (
        rows_a, row_halo_a, row_slots_a, send_rows_a, recv_row_halo_a, recv_row_slot_a
    )
    partial_rows = (rows_p, *adjoint_rows[1:])

    outgoings = {
        id(strips_f): far_f, id(strips_p): far_p, id(rows_f): far_rows_f, id(rows_p): far_rows_p
    }

    def gather_far(strips):
        outgoing = outgoings[id(strips)]
        outgoing[0] = strips[own_edge]
        outgoing[1] = strips[column_edge]

    def keep_own(strips, slots):
        outgoing = outgoings[id(strips)]

        @pl.when(middle)
        def _():
            slots[own_slot] = outgoing[0]

        @pl.when(corner)
        def _():
            slots[2 * own_corner] = outgoing[0]
            slots[2 * own_corner + 1] = outgoing[1]

    def with_levels(strip, rows, stride, index, is_adjoint):
        if is_adjoint:
            for other in range(1, faces):
                strip = jnp.where(sub == 4 + other, rows[stride * other + index], strip)
            return strip
        beneath = jnp.zeros((1, LANES), jnp.float32)
        for other in range(faces - 1):
            beneath = beneath + jnp.where(level > other, rows[stride * other + index], 0.0)
        return strip + jnp.where(sub == 4, rolled(strip, -1, 0) * beneath, 0.0)

    for copy in taken[:2]:
        copy.wait()
    probe_h = per_probe(2)
    spread_h = per_panel(lambda f: spread_ref[2, 0, f])
    h = spread_h * probe_h
    column_f[...] = h
    rows_f[0] = h[0:1, :]
    rows_f[1] = h[SUBLANES - 1 : SUBLANES, :]
    low, high = columns_of((h,))
    rows_f[2] = low[0:1, :]
    rows_f[3] = high[0:1, :]
    gather_far(rows_f)
    probe_z, probe_m, probe_t = per_probe(0), per_probe(1), per_probe(3)
    spread_z, spread_m, spread_t = [
        per_panel(lambda f, c=c: spread_ref[c, 0, f]) for c in (0, 1, 3)
    ]
    for copy in taken[2:]:
        copy.wait()
    u, v = [per_panel(lambda f, c=c: wind_ref[c, 0, f]) for c in range(2)]
    mass = per_panel(lambda f: mass_ref[0, f])
    heat = per_panel(lambda f: heat_ref[0, f])
    var_z, var_m, var_h, var_t = [
        per_panel(lambda f, c=c: variance_ref[c, 0, f]) for c in range(4)
    ]
    z, m, t = spread_z * probe_z, spread_m * probe_m, spread_t * probe_t
    fx = u * h + mass * z
    fy = v * h + mass * m

    def links_of(edge, part, is_row):
        zero = jnp.zeros((SUBLANES, LANES), jnp.int32)
        source = flip = slot = normal = tangent = zero
        for f in range(panels):
            here = panel_of == f
            entries = [links_ref[f, edge, 3 + i] for i in range(4)]
            first, second = entries[0] + entries[1], entries[2] + entries[3]
            turned = links_ref[f, edge, 2]
            far_edge, far_part = links_ref[f, edge, 1], jnp.where(turned == 1, 1 - part, part)
            at_corner = jnp.where(
                far_edge < 2, far_edge * 4 + far_part * 2, far_edge * 2 + far_part * 4 - 3
            )
            held = jnp.where(corner, at_corner, far_edge * 2 + far_part)
            source = jnp.where(here, links_ref[f, edge, 0], source)
            flip = jnp.where(here, turned, flip)
            slot = jnp.where(here, held, slot)
            normal = jnp.where(here, first if is_row else second, normal)
            tangent = jnp.where(here, second if is_row else first, tangent)
        shifted = base + SUBLANES * (source - panel_of)

        def index_of(along):
            index = shifted + jnp.where(flip == 1, SUBLANES - 1 - along, along)
            return jnp.where(lane < SUBLANES * panels * probe_count, index, lane)

        straight = index_of(inner)
        index = straight if is_row else index_of(skew)
        normal, tangent = normal.astype(jnp.float32), tangent.astype(jnp.float32)
        wind = jnp.where(sub == 0, normal, jnp.where(sub == 1, tangent, 1.0))
        ahead = jnp.where(sub == 2, normal, jnp.where(sub == 6, tangent, wind))
        back = jnp.where(
            sub == 1, normal * tangent, jnp.where((sub == 0) | (sub == 3), 1.0, normal)
        )
        return index, slot, ahead, back, straight, wind

    def ghost_across(slots, row_slots, links, is_adjoint, straight=False):
        slot = links[1]
        index = links[4] if straight else links[0]
        strip = nothing
        for number in range(8):
            held = slots[number, 0:SUBLANES]
            if row_slots is not None:
                held = with_levels(held, row_slots, 8, number, is_adjoint)
            strip = jnp.where(slot == number, gathered(held, index, 1), strip)
        return strip * (links[3] if is_adjoint else links[2])

    def coefs_across(links):
        strip = nothing
        for number in range(8):
            held = slots_f[number, SUBLANES : 2 * SUBLANES]
            strip = jnp.where(links[1] == number, gathered(held, links[4], 1), strip)
        return strip * links[5]

    def ghosts_of(buffers, rows_buffers, row_tile, column_tile, is_adjoint):
        halo = buffers[1]
        tiles = []
        for d in range(4):
            strip = halo[d]
            if rows_buffers is not None:
                strip = with_levels(strip, rows_buffers[1], 4, d, is_adjoint)
            if d < 2:
                tiles.append(jnp.where(at[d], row_tile, strip))
            else:
                tiles.append(jnp.where(at[d], column_tile, gathered(strip, base + skew, 1)))
        return tiles

    def tile_of(rows):
        tile = nothing
        for c, value in enumerate(rows):
            tile = jnp.where(sub == c, value, tile)
        return tile

    def correction_of(side, edge, low, corner_low, end, far_end, opposite):
        half_step = jnp.where(low, -0.5 * time_increment, 0.5 * time_increment)
        wind, side_wind, var_n, var_s, var_d, var_w = [
            coefs[side, c : c + 1] for c in range(6)
        ]
        normal, tangent, flux, warmth = [strips_f[edge, c : c + 1] for c in range(4)]
        potential = strips_p[edge, 5:6]
        parts = (
            potential + wind * normal,
            wind * tangent,
            flux,
            wind * warmth,
        )
        turned[side] = gathered(opposite, base + far_end, 1)
        sign = jnp.where(at[0] == at[2], 1.0, -1.0)
        corner_step = jnp.where(corner_low, 0.5 * time_increment, -0.5 * time_increment)
        normal = sign * turned[side, 0:1]
        tangent = -sign * turned[side, 1:2]
        flux = -sign * turned[side, 6:7]
        warmth, potential = turned[side, 3:4], turned[side, 4:5]
        corner_parts = (
            side_wind * normal,
            potential + side_wind * tangent,
            flux,
            side_wind * warmth,
        )
        here = (inner[0:1] == end) & corner
        normal, tangent, depth, warmth = [
            factor * (half_step * part + jnp.where(here, corner_step * extra, 0.0))
            for factor, part, extra in zip((var_n, var_s, var_d, var_w), parts, corner_parts)
        ]
        return tile_of((wind * normal, wind * tangent, normal, depth, wind * warmth))

    def slopes_of(ghosts, x_fields, y_fields):
        low, high = ghosts[0], ghosts[1]
        east = []
        for c, field in enumerate(x_fields):
            before = jnp.where(sub == 0, low[c : c + 1, :], rolled(field, 1, 0))
            after = jnp.where(sub == SUBLANES - 1, high[c : c + 1, :], rolled(field, -1, 0))
            east.append(0.5 * (after - before))
        low, high = gathered(ghosts[2], skew, 0), gathered(ghosts[3], skew, 0)
        north = []
        for c, field in enumerate(y_fields):
            place = base + (sub + c) % SUBLANES
            before = jnp.where(inner == 0, gathered(low, place, 1), rolled(field, 1, 1))
            after = jnp.where(
                inner == SUBLANES - 1, gathered(high, place, 1), rolled(field, -1, 1)
            )
            north.append(0.5 * (after - before))
        return east, north

    geo = t + heat * h
    write_strips(strips_f, (z, m, fx, t, geo, heat, fy, h), (m, z, fy, t, geo, heat, fx, h))
    write_strips(
        strips_f,
        (u, v, var_z, var_m, var_h, var_t),
        (v, u, var_m, var_z, var_h, var_t),
        SUBLANES,
    )
    gather_far(strips_f)
    pl.semaphore_wait(barrier, expected)
    for other in range(1, faces):
        @pl.when(level < other)
        def _():
            below_copy(other, level).start()
            send_near(forward_rows, other)
    send_near(forward)
    send_far(forward)
    for other in range(1, faces):
        @pl.when(level < other)
        def _():
            send_far(forward_rows, other)

    keep_own(strips_f, slots_f)
    row_links = links_of(row_edge, row_part, True)
    column_links = links_of(column_edge, column_part, False)

    def image_of(ghosts):
        east, north = slopes_of(ghosts, (z, m, fx, t, geo), (m, z, fy, t, geo))
        zc = var_z * (z - time_increment * (east[4] + u * east[0] + v * north[1]))
        mc = var_m * (m - time_increment * (north[4] + u * east[1] + v * north[0]))
        hc = var_h * (h - time_increment * (east[2] + north[2]))
        tc = var_t * (t - time_increment * (u * east[3] + v * north[3]))
        x_fields = (u * zc, u * mc, zc, hc, u * tc)
        y_fields = (v * mc, v * zc, mc, hc, v * tc)
        return zc, mc, hc, tc, x_fields, y_fields

    each_wait(forward, False, False)
    for other in range(faces - 1):
        @pl.when(level > other)
        def _():
            below_copy(other, other).wait_recv()

    for other in range(faces - 1):
        geo = geo + heat * jnp.where(level > other, below_ref[other], 0.0)

    def write_rows(rows, tiles):
        zonal, meridional = image_of(tiles)[:2]
        rows[0], rows[1] = zonal[0:1], zonal[SUBLANES - 1 : SUBLANES]
        low, high = columns_of((meridional,))
        rows[2], rows[3] = low[0:1], high[0:1]
        return zonal, meridional

    @pl.when(level > 0)
    def _():
        write_rows(rows_p, ghosts_of(forward, None, nothing, nothing, False))
        gather_far(rows_p)

    for other in range(faces):
        @pl.when(level > other)
        def _():
            send_far(partial_rows, other)

    for other in range(faces - 1):
        @pl.when(level > other)
        def _():
            each_wait(forward_rows, False, False, other)

    ghosts = ghosts_of(forward, forward_rows, nothing, nothing, False)
    x_fields, y_fields = image_of(ghosts)[4:]
    write_strips(strips_p, x_fields + (geo,), y_fields + (geo,))
    gather_far(strips_p)
    send_far(partial)
    keep_own(strips_p, slots_a)

    each_wait(forward, False, True)
    row_end = jnp.where(at[0], 0, SUBLANES - 1)
    column_end = jnp.where(at[2], 0, SUBLANES - 1)

    def with_far(rows):
        row_tile = ghost_across(slots_f, rows, row_links, False)
        column_tile = ghost_across(slots_f, rows, column_links, False)
        return row_tile, [
            jnp.where(at[d], row_tile if d < 2 else column_tile, ghosts[d]) for d in range(4)
        ]

    def corrections(rows, row_tile):
        coefs[0], coefs[1] = coefs_across(row_links), coefs_across(column_links)
        straight_tile = ghost_across(slots_f, rows, column_links, False, True)
        return (
            straight_tile,
            correction_of(0, row_edge, at[0], at[2], column_end, row_end, straight_tile),
            correction_of(1, column_edge, at[2], at[0], row_end, column_end, row_tile),
        )

    @pl.when(level > 0)
    def _():
        row_tile, tiles = with_far(None)
        zonal, meridional = write_rows(rows_a, tiles)
        column_a[0], column_a[1], column_a[2] = zonal, meridional, heat

    for other in range(faces):
        @pl.when(level > other)
        def _():
            send_near(adjoint_rows, other)
            above_copy(other, level).start()

    @pl.when(level > 0)
    def _():
        row_tile = ghost_across(slots_f, None, row_links, False)
        straight_tile, row_fix, column_fix = corrections(None, row_tile)
        row_step = jnp.where(at[0], 0.5 * time_increment, -0.5 * time_increment)
        column_step = jnp.where(at[2], 0.5 * time_increment, -0.5 * time_increment)
        kept[...] = tile_of((
            row_fix[2:3],
            column_fix[2:3],
            row_step * strips_f[row_edge, 10:11] * row_tile[5:6],
            column_step * strips_f[column_edge, 10:11] * straight_tile[5:6],
        ))

    for other in range(faces):
        @pl.when(level > other)
        def _():
            kept_copy(other, level).start()

    for other in range(faces - 1):
        @pl.when(level > other)
        def _():
            each_wait(forward_rows, False, True, other)

    row_tile, ghosts = with_far(row_slots_f)
    zc, mc, hc, tc, x_fields, y_fields = image_of(ghosts)
    write_strips(strips_a, x_fields, y_fields)
    send_near(adjoint)
    straight_tile, row_correction, column_correction = corrections(row_slots_f, row_tile)
    depth_row, depth_column = row_tile[7:8], straight_tile[7:8]

    for far in (False, True):
        each_wait(forward, True, far)
        each_wait(partial if far else adjoint, True, far)
    for other in range(faces):
        @pl.when(level < other)
        def _():
            below_copy(other, level).wait_send()
            for far in (False, True):
                each_wait(forward_rows, True, far, other)

        @pl.when(level > other)
        def _():
            above_copy(other, level).wait_send()
            kept_copy(other, level).wait_send()
            for far in (False, True):
                each_wait(adjoint_rows, True, far, other)

    each_wait(adjoint, False, False)
    each_wait(adjoint, False, True)
    for other in range(1, faces):
        @pl.when(level < other)
        def _():
            above_copy(other, other).wait_recv()
            kept_copy(other, other).wait_recv()
            each_wait(adjoint_rows, False, False, other)
            each_wait(adjoint_rows, False, True, other)

    def with_kept(side, tile):
        for other in range(1, faces):
            upper = kept_ref[other, side : side + 1]
            tile = jnp.where((sub == 4 + other) & (level < other), upper, tile)
        return tile

    row_tile = ghost_across(slots_a, row_slots_a, row_links, True)
    column_tile = ghost_across(slots_a, row_slots_a, column_links, True)
    ghosts = ghosts_of(
        adjoint,
        adjoint_rows,
        row_tile + with_kept(0, row_correction),
        column_tile + gathered(with_kept(1, column_correction), base + skew, 1),
        True,
    )
    above = []
    for other in range(1, faces):
        zonal, meridional = above_ref[other, 0], above_ref[other, 1]
        extra = kept_ref[other, 2:3] * depth_row
        zonal = zonal + jnp.where((sub == row_end) & on_row, extra, 0.0)
        extra = jnp.broadcast_to(kept_ref[other, 3:4] * depth_column, (SUBLANES, LANES))
        extra = gathered(extra, base + sub, 1)
        meridional = meridional + jnp.where((inner == column_end) & on_column, extra, 0.0)
        above.append((zonal, meridional, above_ref[other, 2]))

    east, north = slopes_of(
        ghosts,
        x_fields + tuple(tiles[0] for tiles in above),
        y_fields + tuple(tiles[1] for tiles in above),
    )
    geo_back = time_increment * (east[2] + north[2])
    load = heat * geo_back
    for other, tiles in enumerate(above, 1):
        upper = tiles[2] * (time_increment * (east[4 + other] + north[4 + other]))
        load = load + jnp.where(level < other, upper, 0.0)

    flux_east = time_increment * east[3]
    flux_north = time_increment * north[3]
    z_back = zc + time_increment * (east[0] + north[1]) + mass * flux_east
    m_back = mc + time_increment * (east[1] + north[0]) + mass * flux_north
    t_back = tc + time_increment * (east[4] + north[4]) + geo_back
    h_back = hc + u * flux_east + v * flux_north + load
    out_ref[0] = probe_z + spread_z * z_back
    out_ref[1] = probe_m + spread_m * m_back
    out_ref[2] = probe_h + spread_h * h_back
    out_ref[3] = probe_t + spread_t * t_back


def unpack_kernel(packed_ref, out_ref):
    probe_count, components, _, panels, _, _ = out_ref.shape
    for component in range(components):
        tile = packed_ref[component]
        for p in range(probe_count):
            for f in range(panels):
                start = (p * panels + f) * SUBLANES
                out_ref[p, component, 0, f] = tile[:, start : start + SUBLANES]


def fused(count, faces, *operands):
    tile = (SUBLANES, LANES)
    vmem = pl.BlockSpec(memory_space=pltpu.VMEM)
    whole = pl.BlockSpec(memory_space=pl.ANY)
    probes = operands[0]
    strips = pltpu.VMEM((4, *tile), jnp.float32)
    slots = pltpu.VMEM((8, *tile), jnp.float32)

    def edge_rows(number):
        return pltpu.VMEM((number, 1, LANES), jnp.float32)

    dma = pltpu.SemaphoreType.DMA
    packed = pl.pallas_call(
        functools.partial(tile_kernel, count, faces),
        out_shape=pltpu.VMEM((probes.shape[1], *tile), probes.dtype),
        in_specs=[whole] * len(operands),
        out_specs=vmem,
        scratch_shapes=[pltpu.VMEM(x.shape, x.dtype) for x in operands[:-1]]
        + [
            pltpu.SMEM(operands[-1].shape, operands[-1].dtype),
            dma((len(operands),)),
        ]
        + [pltpu.VMEM((4, 2 * SUBLANES, LANES), jnp.float32), strips, strips]
        + [pltpu.VMEM(tile, jnp.float32), pltpu.VMEM((faces, *tile), jnp.float32)]
        + [pltpu.VMEM((2, *tile), jnp.float32)] * 2
        + [strips] * 2
        + [pltpu.VMEM((8, 2 * SUBLANES, LANES), jnp.float32), slots]
        + [pltpu.VMEM((faces, *tile), jnp.float32), pltpu.VMEM((faces, 3, *tile), jnp.float32)]
        + [pltpu.VMEM(tile, jnp.float32), pltpu.VMEM((3, *tile), jnp.float32)]
        + [edge_rows(4)] * 3
        + [pltpu.VMEM((2, 2 * SUBLANES, LANES), jnp.float32), pltpu.VMEM((2, *tile), jnp.float32)]
        + [edge_rows(2)] * 2
        + [edge_rows(4 * faces)] * 2
        + [edge_rows(8 * faces)] * 2
        + [dma((5,))] * 2
        + [dma((4,))] * 2
        + [dma((1,))] * 2
        + [dma((5 * faces,))] * 2
        + [dma((4 * faces,))] * 2
        + [dma((faces,))] * 2
        + [dma((faces,))] * 6,
        compiler_params=pltpu.CompilerParams(collective_id=0, has_side_effects=True),
    )(*operands)
    return pl.pallas_call(
        unpack_kernel,
        out_shape=jax.ShapeDtypeStruct(probes.shape, probes.dtype),
        in_specs=[vmem],
        out_specs=vmem,
        compiler_params=pltpu.CompilerParams(vmem_limit_bytes=VMEM_BYTES),
    )(packed)


def solution(mesh):
    count, faces = mesh.shape["tx"], mesh.shape["face"]

    def chosen(*operands):
        probe_count, _, levels, panels, rows, columns = operands[0].shape
        fits = (
            levels == 1
            and count == mesh.shape["ty"]
            and count % 2 == 0
            and rows == columns == SUBLANES
            and faces == 2
            and probe_count * panels * SUBLANES < LANES
        )
        return fused(count, faces, *operands) if fits else body(*operands)

    return jax.shard_map(
        chosen,
        mesh=mesh,
        in_specs=(
            P(None, None, "face", None, "tx", "ty"),
            P(None, "face", None, "tx", "ty"),
            P("face", None, "tx", "ty"),
            P("face", None, "tx", "ty"),
            P(None, "face", None, "tx", "ty"),
            P(None, "face", None, "tx", "ty"),
            P(),
        ),
        out_specs=P(None, None, "face", None, "tx", "ty"),
        check_vma=False,
    )
```

```python
import functools

import jax
import jax.numpy as jnp
from jax import lax
from jax.experimental import pallas as pl
from jax.experimental.pallas import tpu as pltpu
from jax.sharding import PartitionSpec as P

MESH = pl.DeviceIdType.MESH
SUBLANES = 8
LANES = 128
VMEM_BYTES = 4 * 2**20

time_increment = 0.3
forward_layout = (("vector", 0), ("vector", 2), ("scalar", 4), ("scalar", 5))
adjoint_layout = (("tensor", 0), ("vector", 4), ("scalar", 6), ("vector", 7))


def padded_2(array, sides, width):
    for axis, dim in sides:
        devices, length = (lax.axis_size(axis), array.shape[dim])
        up = [(i, (i + 1) % devices) for i in range(devices - 1)]
        down = [(j, i) for i, j in up]
        last = lax.slice_in_dim(array, length - width, length, axis=dim)
        leading = lax.slice_in_dim(array, 0, width, axis=dim)
        before = lax.ppermute(last, axis, up)
        after = lax.ppermute(leading, axis, down)
        array = jnp.concatenate([before, array, after], axis=dim)
    return array


def carried_in(value, axis, join, neutral, backward):
    count, mine = (lax.axis_size(axis), lax.axis_index(axis))
    pieces = lax.all_gather(value, axis)
    if backward:
        pieces = pieces[::-1]
        mine = count - 1 - mine
    total = jnp.full_like(value, 0) + jnp.asarray(neutral, value.dtype)

    def hop(position, total):
        longer = join(total, pieces[position])
        return jnp.where(position < mine, longer, total)

    return lax.fori_loop(0, count - 1, hop, total)


def carry_pair(leading, trailing, entries):
    return (
        entries[0] * leading + entries[1] * trailing,
        entries[2] * leading + entries[3] * trailing,
    )


def rotate_edge(edge_strip, matrix_codes, layout):
    matrix = matrix_codes.astype(edge_strip.dtype)
    entries = [matrix[:, column].reshape(1, 1, 6, 1) for column in range(4)]
    channels = [edge_strip[number] for number in range(edge_strip.shape[0])]
    for species, offset in layout:
        if species == "vector":
            channels[offset], channels[offset + 1] = carry_pair(
                channels[offset], channels[offset + 1], entries
            )
        elif species == "tensor":
            channels[offset], channels[offset + 1] = carry_pair(
                channels[offset], channels[offset + 1], entries
            )
            channels[offset + 2], channels[offset + 3] = carry_pair(
                channels[offset + 2], channels[offset + 3], entries
            )
            channels[offset], channels[offset + 2] = carry_pair(
                channels[offset], channels[offset + 2], entries
            )
            channels[offset + 1], channels[offset + 3] = carry_pair(
                channels[offset + 1], channels[offset + 3], entries
            )
    return jnp.stack(channels)


def orient(edge_rows, face_links, side, layout):
    lines = edge_rows.reshape(edge_rows.shape[:3] + (-1, edge_rows.shape[5]))
    sides = edge_rows.shape[4]
    chosen = jnp.concatenate(
        [
            lax.dynamic_slice_in_dim(
                lines, face_links[f, side, 0] * sides + face_links[f, side, 1], 1, 3
            )
            for f in range(face_links.shape[0])
        ],
        axis=3,
    )
    flipped = (face_links[:, side, 2] == 1).reshape(1, 1, 1, 6, 1)
    chosen = jnp.where(flipped, chosen[..., ::-1], chosen)
    return rotate_edge(chosen, face_links[:, side, 3:7], layout)


def face_rows(fields):
    tile_row = lax.axis_index("tx")
    tile_column = lax.axis_index("ty")
    low_rows = jnp.where(tile_row == 0, fields[..., 0, :], 0.0)
    high_rows = jnp.where(tile_row == lax.axis_size("tx") - 1, fields[..., -1, :], 0.0)
    low_columns = jnp.where(tile_column == 0, fields[..., :, 0], 0.0)
    high_columns = jnp.where(tile_column == lax.axis_size("ty") - 1, fields[..., :, -1], 0.0)
    row_pair = jnp.stack([low_rows, high_rows], axis=4)
    column_pair = jnp.stack([low_columns, high_columns], axis=4)
    row_full = lax.psum(lax.all_gather(row_pair, "ty", axis=5, tiled=True), "tx")
    column_full = lax.psum(lax.all_gather(column_pair, "tx", axis=5, tiled=True), "ty")
    return jnp.concatenate([row_full, column_full], axis=4)


def extended_slopes(fields, face_links, layout):
    row_cells = fields.shape[4]
    column_cells = fields.shape[5]
    tile_row = lax.axis_index("tx")
    tile_column = lax.axis_index("ty")
    padded = padded_2(fields, (("tx", 4), ("ty", 5)), 1)
    edge_rows = face_rows(fields)
    western = lax.dynamic_slice_in_dim(
        orient(edge_rows, face_links, 0, layout), tile_column * column_cells, column_cells, 4
    )
    eastern = lax.dynamic_slice_in_dim(
        orient(edge_rows, face_links, 1, layout), tile_column * column_cells, column_cells, 4
    )
    southern = lax.dynamic_slice_in_dim(
        orient(edge_rows, face_links, 2, layout), tile_row * row_cells, row_cells, 4
    )
    northern = lax.dynamic_slice_in_dim(
        orient(edge_rows, face_links, 3, layout), tile_row * row_cells, row_cells, 4
    )
    row_number = lax.broadcasted_iota(jnp.int32, (row_cells, column_cells), 0)
    column_number = lax.broadcasted_iota(jnp.int32, (row_cells, column_cells), 1)
    first_row = (row_number == 0) & (tile_row == 0)
    last_row = (row_number == row_cells - 1) & (tile_row == lax.axis_size("tx") - 1)
    first_column = (column_number == 0) & (tile_column == 0)
    last_column = (column_number == column_cells - 1) & (tile_column == lax.axis_size("ty") - 1)
    east_slope_derivative = 0.5 * (padded[..., 2:, 1:-1] - padded[..., :-2, 1:-1])
    east_slope_derivative = (
        east_slope_derivative
        + jnp.where(last_row, 0.5 * eastern[..., None, :], 0.0)
        - jnp.where(first_row, 0.5 * western[..., None, :], 0.0)
    )
    north_slope_derivative = 0.5 * (padded[..., 1:-1, 2:] - padded[..., 1:-1, :-2])
    north_slope_derivative = (
        north_slope_derivative
        + jnp.where(last_column, 0.5 * northern[..., :, None], 0.0)
        - jnp.where(first_column, 0.5 * southern[..., :, None], 0.0)
    )
    return (east_slope_derivative, north_slope_derivative)


def pressure_of(sheet_depth_state):
    within = jnp.cumsum(sheet_depth_state, axis=1)
    totals_here = within[:, -1]
    underneath = carried_in(totals_here, "face", jnp.add, jnp.zeros_like(totals_here), False)
    return within + underneath[:, None]


def load_of(sensitivity):
    within = jnp.flip(jnp.cumsum(jnp.flip(sensitivity, 1), axis=1), 1)
    totals_here = within[:, 0]
    overhead = carried_in(totals_here, "face", jnp.add, jnp.zeros_like(totals_here), True)
    return within + overhead[:, None]


def body(
    probes,
    background_wind,
    layer_mass,
    trajectory_heat_factor,
    spread,
    inverse_misfit_variance,
    face_links,
):
    normalised_state_array = spread[None] * probes
    west_east_wind_part, south_north_wind_speed, sheet_depth_state, sheet_warmth_state = (
        normalised_state_array[:, 0],
        normalised_state_array[:, 1],
        normalised_state_array[:, 2],
        normalised_state_array[:, 3],
    )
    east_wind_speed, north_wind_speed = (background_wind[0], background_wind[1])
    ground_barometric_load = pressure_of(sheet_depth_state)
    gravity_potential_level = sheet_warmth_state + trajectory_heat_factor * ground_barometric_load
    east_mass_transport = east_wind_speed * sheet_depth_state + layer_mass * west_east_wind_part
    north_mass_transport = (
        north_wind_speed * sheet_depth_state + layer_mass * south_north_wind_speed
    )
    joined_state_arrays = jnp.stack(
        [
            west_east_wind_part,
            south_north_wind_speed,
            east_mass_transport,
            north_mass_transport,
            sheet_warmth_state,
            gravity_potential_level,
        ]
    )
    east_slope_derivative, north_slope_derivative = extended_slopes(
        joined_state_arrays, face_links, forward_layout
    )
    west_east_wind_after = west_east_wind_part - time_increment * (
        east_slope_derivative[5]
        + east_wind_speed * east_slope_derivative[0]
        + north_wind_speed * north_slope_derivative[0]
    )
    south_north_wind_after = south_north_wind_speed - time_increment * (
        north_slope_derivative[5]
        + east_wind_speed * east_slope_derivative[1]
        + north_wind_speed * north_slope_derivative[1]
    )
    depth_after_update = sheet_depth_state - time_increment * (
        east_slope_derivative[2] + north_slope_derivative[3]
    )
    warmth_after_update = sheet_warmth_state - time_increment * (
        east_wind_speed * east_slope_derivative[4] + north_wind_speed * north_slope_derivative[4]
    )
    zonal_cost = inverse_misfit_variance[0] * west_east_wind_after
    meridional_cost = inverse_misfit_variance[1] * south_north_wind_after
    thickness_cost = inverse_misfit_variance[2] * depth_after_update
    heat_misfit_penalty = inverse_misfit_variance[3] * warmth_after_update
    sensitive = jnp.stack(
        [
            east_wind_speed * zonal_cost,
            east_wind_speed * meridional_cost,
            north_wind_speed * zonal_cost,
            north_wind_speed * meridional_cost,
            zonal_cost,
            meridional_cost,
            thickness_cost,
            east_wind_speed * heat_misfit_penalty,
            north_wind_speed * heat_misfit_penalty,
        ]
    )
    east_slope_derivative, north_slope_derivative = extended_slopes(
        sensitive, face_links, adjoint_layout
    )
    geo_back = time_increment * (east_slope_derivative[4] + north_slope_derivative[5])
    flux_east_back = time_increment * east_slope_derivative[6]
    flux_north_back = time_increment * north_slope_derivative[6]
    zonal_back = (
        zonal_cost
        + time_increment * (east_slope_derivative[0] + north_slope_derivative[2])
        + layer_mass * flux_east_back
    )
    meridional_back = (
        meridional_cost
        + time_increment * (east_slope_derivative[1] + north_slope_derivative[3])
        + layer_mass * flux_north_back
    )
    warmth_back = (
        heat_misfit_penalty
        + time_increment * (east_slope_derivative[7] + north_slope_derivative[8])
        + geo_back
    )
    thickness_back = (
        thickness_cost
        + east_wind_speed * flux_east_back
        + north_wind_speed * flux_north_back
        + load_of(trajectory_heat_factor * geo_back)
    )
    adjoint_out = jnp.stack([zonal_back, meridional_back, thickness_back, warmth_back], axis=1)
    return probes + spread[None] * adjoint_out


def rolled(tile, shift, axis):
    return pltpu.roll(tile, shift % tile.shape[axis], axis)


def gathered(tile, index, axis):
    return jnp.take_along_axis(tile, index, axis=axis, mode="promise_in_bounds")


def tile_kernel(
    count,
    faces,
    probes_hbm,
    wind_hbm,
    mass_hbm,
    heat_hbm,
    spread_hbm,
    variance_hbm,
    links_hbm,
    out_ref,
    probes_ref,
    wind_ref,
    mass_ref,
    heat_ref,
    spread_ref,
    variance_ref,
    links_ref,
    take_sem,
    strips_f,
    strips_a,
    strips_p,
    kept,
    kept_ref,
    coefs,
    turned,
    halo_f,
    halo_a,
    slots_f,
    slots_a,
    below_ref,
    above_ref,
    column_f,
    column_a,
    rows_f,
    rows_a,
    rows_p,
    far_f,
    far_p,
    far_rows_f,
    far_rows_p,
    row_halo_f,
    row_halo_a,
    row_slots_f,
    row_slots_a,
    send_f,
    send_a,
    recv_halo_f,
    recv_halo_a,
    recv_slot_f,
    recv_slot_a,
    send_rows_f,
    send_rows_a,
    recv_row_halo_f,
    recv_row_halo_a,
    recv_row_slot_f,
    recv_row_slot_a,
    send_below,
    send_above,
    recv_below,
    recv_above,
    send_kept,
    recv_kept,
):
    level = lax.axis_index("face")
    row = lax.axis_index("tx")
    column = lax.axis_index("ty")
    probe_count = probes_ref.shape[0]
    panels = probes_ref.shape[3]
    last = count - 1
    at = [row == 0, row == last, column == 0, column == last]
    on_row = at[0] | at[1]
    on_column = at[2] | at[3]
    corner = on_row & on_column
    middle = (on_row | on_column) & ~corner
    row_edge = jnp.where(at[0], 0, 1)
    column_edge = jnp.where(at[2], 2, 3)
    half = count // 2
    row_part = jnp.where(column < half, 0, 1)
    column_part = jnp.where(row < half, 0, 1)
    row_slot = row_edge * 2 + row_part
    column_slot = column_edge * 2 + column_part
    own_edge = jnp.where(on_row, row_edge, column_edge)
    own_slot = jnp.where(on_row, row_slot, column_slot)
    along = jnp.where(on_row, column, row)
    near = jnp.where(along < half, along, last - along)

    def slot_place(slot):
        edge, part = slot // 2, slot % 2
        segment = near + part * (last - 2 * near)
        return (
            jnp.where(edge < 2, edge * last, segment),
            jnp.where(edge < 2, segment, (edge - 2) * last),
        )

    own_corner = row_edge * 2 + column_edge - 2

    def corner_place(number):
        return (number // 2 * last, number % 2 * last)

    beside = [(row - 1, column), (row + 1, column), (row, column - 1), (row, column + 1)]

    barrier = pltpu.get_barrier_semaphore()

    def greet(other, place):
        pl.semaphore_signal(
            barrier,
            inc=1,
            device_id={"face": other, "tx": place[0], "ty": place[1]},
            device_id_type=MESH,
        )

    taken = [
        pltpu.make_async_copy(source, target, take_sem.at[i])
        for i, (source, target) in enumerate(
            (
                (probes_hbm, probes_ref),
                (spread_hbm, spread_ref),
                (wind_hbm, wind_ref),
                (mass_hbm, mass_ref),
                (heat_hbm, heat_ref),
                (variance_hbm, variance_ref),
                (links_hbm, links_ref),
            )
        )
    ]
    for copy in taken:
        copy.start()

    @pl.when(middle)
    def _():
        for step in range(1, faces):
            for slot in range(8):
                greet((level + step) % faces, slot_place(slot))
        for step in range(1, 8):
            greet(level, slot_place((own_slot + step) % 8))

    @pl.when(corner)
    def _():
        for step in range(1, faces):
            for number in range(4):
                greet((level + step) % faces, corner_place(number))
        for step in range(1, 4):
            greet(level, corner_place((own_corner + step) % 4))

    for d in range(4):
        @pl.when(~at[d])
        def _():
            for other in range(faces):
                greet(other, beside[d])

    for step in range(1, faces):
        greet((level + step) % faces, (row, column))

    expected = (
        faces - 1 + jnp.where(middle, 8 * faces - 1, 0) + jnp.where(corner, 4 * faces - 1, 0)
    )
    for d in range(4):
        expected = expected + jnp.where(at[d], 0, faces)

    sub = lax.broadcasted_iota(jnp.int32, (SUBLANES, LANES), 0)
    lane = lax.broadcasted_iota(jnp.int32, (SUBLANES, LANES), 1)
    inner = lane % SUBLANES
    panel_of = (lane // SUBLANES) % panels
    base = lane - inner
    skew = (inner - sub + SUBLANES) % SUBLANES
    unskew = base + (inner + sub) % SUBLANES

    def packed(tiles):
        width = LANES - SUBLANES * len(tiles)
        return jnp.concatenate(tiles + [jnp.zeros((SUBLANES, width), jnp.float32)], axis=1)

    def per_panel(load):
        return packed([load(f) for f in range(panels)] * probe_count)

    def per_probe(component):
        return packed(
            [
                probes_ref[p, component, 0, f]
                for p in range(probe_count)
                for f in range(panels)
            ]
        )

    def level_copy(other, source, target, send, recv):
        return pltpu.make_async_remote_copy(
            src_ref=source,
            dst_ref=target,
            send_sem=send,
            recv_sem=recv,
            device_id={"face": other},
            device_id_type=MESH,
        )

    def below_copy(other, slot):
        return level_copy(
            other, column_f, below_ref.at[slot], send_below.at[other], recv_below.at[slot]
        )

    def above_copy(other, slot):
        return level_copy(
            other, column_a, above_ref.at[slot], send_above.at[other], recv_above.at[slot]
        )

    def kept_copy(other, slot):
        return level_copy(
            other, kept, kept_ref.at[slot], send_kept.at[other], recv_kept.at[slot]
        )

    nothing = jnp.zeros((SUBLANES, LANES), jnp.float32)

    def columns_of(y_fields):
        low = high = nothing
        for c, field in enumerate(y_fields):
            low = jnp.where(skew == c, gathered(field, base, 1), low)
            high = jnp.where(skew == c, gathered(field, base + (SUBLANES - 1), 1), high)
        return [gathered(gathered(tile, skew, 0), unskew, 1) for tile in (low, high)]

    def write_strips(strips, x_fields, y_fields, first=0):
        low = high = nothing
        for c, field in enumerate(x_fields):
            low = jnp.where(sub == c, field[0:1, :], low)
            high = jnp.where(sub == c, field[SUBLANES - 1 : SUBLANES, :], high)
        tiles = (low, high, *columns_of(y_fields))
        for d, tile in enumerate(tiles):
            strips[d, first : first + SUBLANES] = tile

    def strip_copy(source, target, send, recv, other, place):
        return pltpu.make_async_remote_copy(
            src_ref=source,
            dst_ref=target,
            send_sem=send,
            recv_sem=recv,
            device_id={"face": other, "tx": place[0], "ty": place[1]},
            device_id_type=MESH,
        )

    def send_far(buffers, target=None):
        strips, halo, slots, send_sem, recv_halo, recv_slot = buffers
        across = target is not None
        other = target if across else level
        first_send = 5 * target if across else 0
        first_slot = 8 * level if across else 0
        group = level if across else 0

        outgoing = outgoings[id(strips)]

        def send(number, slot, place):
            strip_copy(
                outgoing.at[pl.ds(0, number)],
                slots.at[pl.ds(first_slot + slot, number)],
                send_sem.at[first_send + 4],
                recv_slot.at[group],
                other,
                place,
            ).start()

        @pl.when(middle)
        def _():
            for step in range(0 if across else 1, 8):
                send(1, own_slot, slot_place((own_slot + step) % 8))

        @pl.when(corner)
        def _():
            for step in range(0 if across else 1, 4):
                send(2, 2 * own_corner, corner_place((own_corner + step) % 4))

    def send_near(buffers, target=None):
        strips, halo, slots, send, recv_halo, recv_slot = buffers
        across = target is not None
        other = target if across else level
        first_send = 5 * target if across else 0
        first_halo = 4 * level if across else 0
        for d in range(4):
            @pl.when(~at[d])
            def _():
                strip_copy(
                    strips.at[d, pl.ds(0, halo.shape[1])],
                    halo.at[first_halo + (d ^ 1)],
                    send.at[first_send + d],
                    recv_halo.at[first_halo + (d ^ 1)],
                    other,
                    beside[d],
                ).start()

    def each_wait(buffers, sent, far, other=None):
        strips, halo, slots, send, recv_halo, recv_slot = buffers
        across = other is not None
        first_send = 5 * other if across else 0
        first_halo = 4 * other if across else 0
        group = other if across else 0

        def ended(ref, send_sem, recv_sem):
            copy = strip_copy(ref, ref, send_sem, recv_sem, level, (row, column))
            if sent:
                copy.wait_send()
            else:
                copy.wait_recv()

        if not far:
            for d in range(4):
                @pl.when(~at[d])
                def _():
                    ended(halo.at[0], send.at[first_send + d], recv_halo.at[first_halo + d])

            return
        for role, number in ((middle, 8 if across else 7), (corner, 8 if across else 6)):
            @pl.when(role)
            def _():
                ended(
                    slots.at[pl.ds(0, number)], send.at[first_send + 4], recv_slot.at[group]
                )

    forward = (strips_f, halo_f, slots_f, send_f, recv_halo_f, recv_slot_f)
    adjoint = (strips_a, halo_a, slots_a, send_a, recv_halo_a, recv_slot_a)
    partial = (strips_p, *adjoint[1:])
    forward_rows = (
        rows_f, row_halo_f, row_slots_f, send_rows_f, recv_row_halo_f, recv_row_slot_f
    )
    adjoint_rows = (
        rows_a, row_halo_a, row_slots_a, send_rows_a, recv_row_halo_a, recv_row_slot_a
    )
    partial_rows = (rows_p, *adjoint_rows[1:])

    outgoings = {
        id(strips_f): far_f, id(strips_p): far_p, id(rows_f): far_rows_f, id(rows_p): far_rows_p
    }

    def gather_far(strips):
        outgoing = outgoings[id(strips)]
        outgoing[0] = strips[own_edge]
        outgoing[1] = strips[column_edge]

    def keep_own(strips, slots):
        outgoing = outgoings[id(strips)]

        @pl.when(middle)
        def _():
            slots[own_slot] = outgoing[0]

        @pl.when(corner)
        def _():
            slots[2 * own_corner] = outgoing[0]
            slots[2 * own_corner + 1] = outgoing[1]

    def with_levels(strip, rows, stride, index, is_adjoint):
        if is_adjoint:
            for other in range(1, faces):
                strip = jnp.where(sub == 4 + other, rows[stride * other + index], strip)
            return strip
        beneath = jnp.zeros((1, LANES), jnp.float32)
        for other in range(faces - 1):
            beneath = beneath + jnp.where(level > other, rows[stride * other + index], 0.0)
        return strip + jnp.where(sub == 4, rolled(strip, -1, 0) * beneath, 0.0)

    for copy in taken[:2]:
        copy.wait()
    probe_h = per_probe(2)
    spread_h = per_panel(lambda f: spread_ref[2, 0, f])
    h = spread_h * probe_h
    column_f[...] = h
    rows_f[0] = h[0:1, :]
    rows_f[1] = h[SUBLANES - 1 : SUBLANES, :]
    low, high = columns_of((h,))
    rows_f[2] = low[0:1, :]
    rows_f[3] = high[0:1, :]
    gather_far(rows_f)
    probe_z, probe_m, probe_t = per_probe(0), per_probe(1), per_probe(3)
    spread_z, spread_m, spread_t = [
        per_panel(lambda f, c=c: spread_ref[c, 0, f]) for c in (0, 1, 3)
    ]
    for copy in taken[2:]:
        copy.wait()
    u, v = [per_panel(lambda f, c=c: wind_ref[c, 0, f]) for c in range(2)]
    mass = per_panel(lambda f: mass_ref[0, f])
    heat = per_panel(lambda f: heat_ref[0, f])
    var_z, var_m, var_h, var_t = [
        per_panel(lambda f, c=c: variance_ref[c, 0, f]) for c in range(4)
    ]
    z, m, t = spread_z * probe_z, spread_m * probe_m, spread_t * probe_t
    fx = u * h + mass * z
    fy = v * h + mass * m

    def links_of(edge, part, is_row):
        zero = jnp.zeros((SUBLANES, LANES), jnp.int32)
        source = flip = slot = normal = tangent = zero
        for f in range(panels):
            here = panel_of == f
            entries = [links_ref[f, edge, 3 + i] for i in range(4)]
            first, second = entries[0] + entries[1], entries[2] + entries[3]
            turned = links_ref[f, edge, 2]
            far_edge, far_part = links_ref[f, edge, 1], jnp.where(turned == 1, 1 - part, part)
            at_corner = jnp.where(
                far_edge < 2, far_edge * 4 + far_part * 2, far_edge * 2 + far_part * 4 - 3
            )
            held = jnp.where(corner, at_corner, far_edge * 2 + far_part)
            source = jnp.where(here, links_ref[f, edge, 0], source)
            flip = jnp.where(here, turned, flip)
            slot = jnp.where(here, held, slot)
            normal = jnp.where(here, first if is_row else second, normal)
            tangent = jnp.where(here, second if is_row else first, tangent)
        shifted = base + SUBLANES * (source - panel_of)

        def index_of(along):
            index = shifted + jnp.where(flip == 1, SUBLANES - 1 - along, along)
            return jnp.where(lane < SUBLANES * panels * probe_count, index, lane)

        straight = index_of(inner)
        index = straight if is_row else index_of(skew)
        normal, tangent = normal.astype(jnp.float32), tangent.astype(jnp.float32)
        wind = jnp.where(sub == 0, normal, jnp.where(sub == 1, tangent, 1.0))
        ahead = jnp.where(sub == 2, normal, jnp.where(sub == 6, tangent, wind))
        back = jnp.where(
            sub == 1, normal * tangent, jnp.where((sub == 0) | (sub == 3), 1.0, normal)
        )
        return index, slot, ahead, back, straight, wind

    def ghost_across(slots, row_slots, links, is_adjoint, straight=False):
        slot = links[1]
        index = links[4] if straight else links[0]
        strip = nothing
        for number in range(8):
            held = slots[number, 0:SUBLANES]
            if row_slots is not None:
                held = with_levels(held, row_slots, 8, number, is_adjoint)
            strip = jnp.where(slot == number, gathered(held, index, 1), strip)
        return strip * (links[3] if is_adjoint else links[2])

    def coefs_across(links):
        strip = nothing
        for number in range(8):
            held = slots_f[number, SUBLANES : 2 * SUBLANES]
            strip = jnp.where(links[1] == number, gathered(held, links[4], 1), strip)
        return strip * links[5]

    def ghosts_of(buffers, rows_buffers, row_tile, column_tile, is_adjoint):
        halo = buffers[1]
        tiles = []
        for d in range(4):
            strip = halo[d]
            if rows_buffers is not None:
                strip = with_levels(strip, rows_buffers[1], 4, d, is_adjoint)
            if d < 2:
                tiles.append(jnp.where(at[d], row_tile, strip))
            else:
                tiles.append(jnp.where(at[d], column_tile, gathered(strip, base + skew, 1)))
        return tiles

    def tile_of(rows):
        tile = nothing
        for c, value in enumerate(rows):
            tile = jnp.where(sub == c, value, tile)
        return tile

    def correction_of(side, edge, low, corner_low, end, far_end, opposite):
        half_step = jnp.where(low, -0.5 * time_increment, 0.5 * time_increment)
        wind, side_wind, var_n, var_s, var_d, var_w = [
            coefs[side, c : c + 1] for c in range(6)
        ]
        normal, tangent, flux, warmth = [strips_f[edge, c : c + 1] for c in range(4)]
        potential = strips_p[edge, 5:6]
        parts = (
            potential + wind * normal,
            wind * tangent,
            flux,
            wind * warmth,
        )
        turned[side] = gathered(opposite, base + far_end, 1)
        sign = jnp.where(at[0] == at[2], 1.0, -1.0)
        corner_step = jnp.where(corner_low, 0.5 * time_increment, -0.5 * time_increment)
        normal = sign * turned[side, 0:1]
        tangent = -sign * turned[side, 1:2]
        flux = -sign * turned[side, 6:7]
        warmth, potential = turned[side, 3:4], turned[side, 4:5]
        corner_parts = (
            side_wind * normal,
            potential + side_wind * tangent,
            flux,
            side_wind * warmth,
        )
        here = (inner[0:1] == end) & corner
        normal, tangent, depth, warmth = [
            factor * (half_step * part + jnp.where(here, corner_step * extra, 0.0))
            for factor, part, extra in zip((var_n, var_s, var_d, var_w), parts, corner_parts)
        ]
        return tile_of((wind * normal, wind * tangent, normal, depth, wind * warmth))

    first_row, last_row = sub == 0, sub == SUBLANES - 1
    first_column, last_column = inner == 0, inner == SUBLANES - 1

    def inside_x(field):
        before = jnp.where(first_row, 0.0, rolled(field, 1, 0))
        return 0.5 * (jnp.where(last_row, 0.0, rolled(field, -1, 0)) - before)

    def inside_y(field):
        before = jnp.where(first_column, 0.0, rolled(field, 1, 1))
        return 0.5 * (jnp.where(last_column, 0.0, rolled(field, -1, 1)) - before)

    def edges_of(ghosts, number):
        low, high = 0.5 * ghosts[0], 0.5 * ghosts[1]
        east = [
            jnp.where(last_row, high[c : c + 1, :], 0.0)
            - jnp.where(first_row, low[c : c + 1, :], 0.0)
            for c in range(number)
        ]
        low, high = [gathered(0.5 * tile, skew, 0) for tile in ghosts[2:]]
        north = []
        for c in range(number):
            place = base + (sub + c) % SUBLANES
            north.append(
                jnp.where(last_column, gathered(high, place, 1), 0.0)
                - jnp.where(first_column, gathered(low, place, 1), 0.0)
            )
        return east, north

    geo = t + heat * h
    write_strips(strips_f, (z, m, fx, t, geo, heat, fy, h), (m, z, fy, t, geo, heat, fx, h))
    write_strips(
        strips_f,
        (u, v, var_z, var_m, var_h, var_t),
        (v, u, var_m, var_z, var_h, var_t),
        SUBLANES,
    )
    gather_far(strips_f)
    pl.semaphore_wait(barrier, expected)
    for other in range(1, faces):
        @pl.when(level < other)
        def _():
            below_copy(other, level).start()
            send_near(forward_rows, other)
    send_near(forward)
    send_far(forward)
    for other in range(1, faces):
        @pl.when(level < other)
        def _():
            send_far(forward_rows, other)

    keep_own(strips_f, slots_f)
    row_links = links_of(row_edge, row_part, True)
    column_links = links_of(column_edge, column_part, False)

    step_z, step_m, step_h, step_t = [
        -time_increment * var for var in (var_z, var_m, var_h, var_t)
    ]

    def change_of(east, north):
        return (
            step_z * (east[4] + u * east[0] + v * north[1]),
            step_m * (north[4] + u * east[1] + v * north[0]),
            step_h * (east[2] + north[2]),
            step_t * (u * east[3] + v * north[3]),
        )

    def plus(tiles, others):
        return [tile + other for tile, other in zip(tiles, others)]

    def sensitive_of(tiles):
        zc, mc, hc, tc = tiles
        return (u * zc, u * mc, zc, hc, u * tc), (v * mc, v * zc, mc, hc, v * tc)

    image = plus(
        (var_z * z, var_m * m, var_h * h, var_t * t),
        change_of(
            [inside_x(field) for field in (z, m, fx, t, geo)],
            [inside_y(field) for field in (m, z, fy, t, geo)],
        ),
    )
    each_wait(forward, False, False)
    for other in range(faces - 1):
        @pl.when(level > other)
        def _():
            below_copy(other, other).wait_recv()

    lower = nothing
    for other in range(faces - 1):
        lower = lower + heat * jnp.where(level > other, below_ref[other], 0.0)
    geo = geo + lower
    image[0] = image[0] + step_z * inside_x(lower)
    image[1] = image[1] + step_m * inside_y(lower)

    def write_rows(rows, tiles):
        zonal, meridional = plus(image, change_of(*edges_of(tiles, 5)))[:2]
        rows[0], rows[1] = zonal[0:1], zonal[SUBLANES - 1 : SUBLANES]
        low, high = columns_of((meridional,))
        rows[2], rows[3] = low[0:1], high[0:1]
        return zonal, meridional

    @pl.when(level > 0)
    def _():
        write_rows(rows_p, ghosts_of(forward, None, nothing, nothing, False))
        gather_far(rows_p)

    for other in range(faces):
        @pl.when(level > other)
        def _():
            send_far(partial_rows, other)

    for other in range(faces - 1):
        @pl.when(level > other)
        def _():
            each_wait(forward_rows, False, False, other)

    ghosts = ghosts_of(forward, forward_rows, nothing, nothing, False)
    image = plus(image, change_of(*edges_of(ghosts, 5)))
    x_fields, y_fields = sensitive_of(image)
    write_strips(strips_p, x_fields + (geo,), y_fields + (geo,))
    gather_far(strips_p)
    send_far(partial)
    keep_own(strips_p, slots_a)

    each_wait(forward, False, True)
    row_end = jnp.where(at[0], 0, SUBLANES - 1)
    column_end = jnp.where(at[2], 0, SUBLANES - 1)

    def with_far(rows):
        row_tile = ghost_across(slots_f, rows, row_links, False)
        column_tile = ghost_across(slots_f, rows, column_links, False)
        return row_tile, [
            jnp.where(at[d], row_tile if d < 2 else column_tile, 0.0) for d in range(4)
        ]

    def corrections(rows, row_tile):
        coefs[0], coefs[1] = coefs_across(row_links), coefs_across(column_links)
        straight_tile = ghost_across(slots_f, rows, column_links, False, True)
        return (
            straight_tile,
            correction_of(0, row_edge, at[0], at[2], column_end, row_end, straight_tile),
            correction_of(1, column_edge, at[2], at[0], row_end, column_end, row_tile),
        )

    @pl.when(level > 0)
    def _():
        row_tile, tiles = with_far(None)
        zonal, meridional = write_rows(rows_a, tiles)
        column_a[0], column_a[1], column_a[2] = zonal, meridional, heat

    for other in range(faces):
        @pl.when(level > other)
        def _():
            send_near(adjoint_rows, other)
            above_copy(other, level).start()

    @pl.when(level > 0)
    def _():
        row_tile = ghost_across(slots_f, None, row_links, False)
        straight_tile, row_fix, column_fix = corrections(None, row_tile)
        row_step = jnp.where(at[0], 0.5 * time_increment, -0.5 * time_increment)
        column_step = jnp.where(at[2], 0.5 * time_increment, -0.5 * time_increment)
        kept[...] = tile_of((
            row_fix[2:3],
            column_fix[2:3],
            row_step * strips_f[row_edge, 10:11] * row_tile[5:6],
            column_step * strips_f[column_edge, 10:11] * straight_tile[5:6],
        ))

    for other in range(faces):
        @pl.when(level > other)
        def _():
            kept_copy(other, level).start()

    for other in range(faces - 1):
        @pl.when(level > other)
        def _():
            each_wait(forward_rows, False, True, other)

    row_tile, ghosts = with_far(row_slots_f)
    zc, mc, hc, tc = plus(image, change_of(*edges_of(ghosts, 5)))
    x_fields, y_fields = sensitive_of((zc, mc, hc, tc))
    write_strips(strips_a, x_fields, y_fields)
    send_near(adjoint)
    straight_tile, row_correction, column_correction = corrections(row_slots_f, row_tile)
    depth_row, depth_column = row_tile[7:8], straight_tile[7:8]

    def back_of(east, north):
        flux_east, flux_north = time_increment * east[3], time_increment * north[3]
        geo_back = time_increment * (east[2] + north[2])
        return (
            time_increment * (east[0] + north[1]) + mass * flux_east,
            time_increment * (east[1] + north[0]) + mass * flux_north,
            u * flux_east + v * flux_north + heat * geo_back,
            time_increment * (east[4] + north[4]) + geo_back,
        )

    spreads = (spread_z, spread_m, spread_h, spread_t)
    inside = back_of([inside_x(x) for x in x_fields], [inside_y(y) for y in y_fields])
    outcome = [
        probe + spread * (own + back)
        for probe, spread, own, back in zip(
            (probe_z, probe_m, probe_h, probe_t), spreads, (zc, mc, hc, tc), inside
        )
    ]

    for far in (False, True):
        each_wait(forward, True, far)
        each_wait(partial if far else adjoint, True, far)
    for other in range(faces):
        @pl.when(level < other)
        def _():
            below_copy(other, level).wait_send()
            for far in (False, True):
                each_wait(forward_rows, True, far, other)

        @pl.when(level > other)
        def _():
            above_copy(other, level).wait_send()
            kept_copy(other, level).wait_send()
            for far in (False, True):
                each_wait(adjoint_rows, True, far, other)

    each_wait(adjoint, False, False)
    each_wait(adjoint, False, True)
    for other in range(1, faces):
        @pl.when(level < other)
        def _():
            above_copy(other, other).wait_recv()
            kept_copy(other, other).wait_recv()
            each_wait(adjoint_rows, False, False, other)
            each_wait(adjoint_rows, False, True, other)

    def with_kept(side, tile):
        for other in range(1, faces):
            upper = kept_ref[other, side : side + 1]
            tile = jnp.where((sub == 4 + other) & (level < other), upper, tile)
        return tile

    row_tile = ghost_across(slots_a, row_slots_a, row_links, True)
    column_tile = ghost_across(slots_a, row_slots_a, column_links, True)
    ghosts = ghosts_of(
        adjoint,
        adjoint_rows,
        row_tile + with_kept(0, row_correction),
        column_tile + gathered(with_kept(1, column_correction), base + skew, 1),
        True,
    )
    east, north = edges_of(ghosts, 4 + faces)
    added = list(back_of(east, north))
    for other in range(1, faces):
        zonal, meridional = above_ref[other, 0], above_ref[other, 1]
        extra = kept_ref[other, 2:3] * depth_row
        zonal = zonal + jnp.where((sub == row_end) & on_row, extra, 0.0)
        extra = jnp.broadcast_to(kept_ref[other, 3:4] * depth_column, (SUBLANES, LANES))
        extra = gathered(extra, base + sub, 1)
        meridional = meridional + jnp.where((inner == column_end) & on_column, extra, 0.0)
        slope = inside_x(zonal) + inside_y(meridional) + east[4 + other] + north[4 + other]
        upper = above_ref[other, 2] * (time_increment * slope)
        added[2] = added[2] + jnp.where(level < other, upper, 0.0)

    for component in range(4):
        out_ref[component] = outcome[component] + spreads[component] * added[component]


def unpack_kernel(packed_ref, out_ref):
    probe_count, components, _, panels, _, _ = out_ref.shape
    for component in range(components):
        tile = packed_ref[component]
        for p in range(probe_count):
            for f in range(panels):
                start = (p * panels + f) * SUBLANES
                out_ref[p, component, 0, f] = tile[:, start : start + SUBLANES]


def fused(count, faces, *operands):
    tile = (SUBLANES, LANES)
    vmem = pl.BlockSpec(memory_space=pltpu.VMEM)
    whole = pl.BlockSpec(memory_space=pl.ANY)
    probes = operands[0]
    strips = pltpu.VMEM((4, *tile), jnp.float32)
    slots = pltpu.VMEM((8, *tile), jnp.float32)

    def edge_rows(number):
        return pltpu.VMEM((number, 1, LANES), jnp.float32)

    dma = pltpu.SemaphoreType.DMA
    packed = pl.pallas_call(
        functools.partial(tile_kernel, count, faces),
        out_shape=pltpu.VMEM((probes.shape[1], *tile), probes.dtype),
        in_specs=[whole] * len(operands),
        out_specs=vmem,
        scratch_shapes=[pltpu.VMEM(x.shape, x.dtype) for x in operands[:-1]]
        + [
            pltpu.SMEM(operands[-1].shape, operands[-1].dtype),
            dma((len(operands),)),
        ]
        + [pltpu.VMEM((4, 2 * SUBLANES, LANES), jnp.float32), strips, strips]
        + [pltpu.VMEM(tile, jnp.float32), pltpu.VMEM((faces, *tile), jnp.float32)]
        + [pltpu.VMEM((2, *tile), jnp.float32)] * 2
        + [strips] * 2
        + [pltpu.VMEM((8, 2 * SUBLANES, LANES), jnp.float32), slots]
        + [pltpu.VMEM((faces, *tile), jnp.float32), pltpu.VMEM((faces, 3, *tile), jnp.float32)]
        + [pltpu.VMEM(tile, jnp.float32), pltpu.VMEM((3, *tile), jnp.float32)]
        + [edge_rows(4)] * 3
        + [pltpu.VMEM((2, 2 * SUBLANES, LANES), jnp.float32), pltpu.VMEM((2, *tile), jnp.float32)]
        + [edge_rows(2)] * 2
        + [edge_rows(4 * faces)] * 2
        + [edge_rows(8 * faces)] * 2
        + [dma((5,))] * 2
        + [dma((4,))] * 2
        + [dma((1,))] * 2
        + [dma((5 * faces,))] * 2
        + [dma((4 * faces,))] * 2
        + [dma((faces,))] * 2
        + [dma((faces,))] * 6,
        compiler_params=pltpu.CompilerParams(collective_id=0, has_side_effects=True),
    )(*operands)
    return pl.pallas_call(
        unpack_kernel,
        out_shape=jax.ShapeDtypeStruct(probes.shape, probes.dtype),
        in_specs=[vmem],
        out_specs=vmem,
        compiler_params=pltpu.CompilerParams(vmem_limit_bytes=VMEM_BYTES),
    )(packed)


def solution(mesh):
    count, faces = mesh.shape["tx"], mesh.shape["face"]

    def chosen(*operands):
        probe_count, _, levels, panels, rows, columns = operands[0].shape
        fits = (
            levels == 1
            and count == mesh.shape["ty"]
            and count % 2 == 0
            and rows == columns == SUBLANES
            and faces == 2
            and probe_count * panels * SUBLANES < LANES
        )
        return fused(count, faces, *operands) if fits else body(*operands)

    return jax.shard_map(
        chosen,
        mesh=mesh,
        in_specs=(
            P(None, None, "face", None, "tx", "ty"),
            P(None, "face", None, "tx", "ty"),
            P("face", None, "tx", "ty"),
            P("face", None, "tx", "ty"),
            P(None, "face", None, "tx", "ty"),
            P(None, "face", None, "tx", "ty"),
            P(),
        ),
        out_specs=P(None, None, "face", None, "tx", "ty"),
        check_vma=False,
    )
```
